32 devices in a mesh: tm: 8 (over y, x, core), space: 4 (over z).
Axes of the slice: x: 2, y: 2, z: 4, core: 2. Of those that a mesh axis runs over, the one named last changes fastest.
Arguments:
- steps: bfloat16 [24, 1024, 1024], P('tm', 'space'), as said below
- lengths: int32 [8], P('tm'), may hold values from 1 to 3, 16 in all
- anchor: bfloat16 [1024, 2048], P(None, 'space'), may hold values from -6 to 6
Outputs:
- panels: float32 [24, 1024, 2048], P('tm', None, 'space')
The draws below stay inside these ranges and needn't reach their ends.
Inputs may be any that keep to these rules, and one draw needn't show every extreme that they name: `steps`: slots of a section beyond its length hold entries that no output reads.
All inputs are finite; a program needn't handle non-finite values. No bound on the sum of `lengths` on one device may be relied on, other than what follows from the above.
Results may differ from the reference program's by a relative error of at most 0.025.
Values may be sent and summed in bfloat16 or wider, within the bound.
A program may use at most 64 MiB of HBM per device.

```python
import math
import jax
import jax.numpy as jnp
import numpy as np
from jax import lax

MESH_NODES = 1024
CAP = 3
COLS = 2048
DAY_SLOTS = 24
N_TM = 8


def draw_steps(key, part):
    intensity_key, noise_random_key, displacement_key, spike_random_key, selection_key = jax.random.split(jax.random.fold_in(key, 11), 5)
    rate_low = 0.004
    rate_high = 0.4
    spread = math.log(rate_high / rate_low)
    mean_inverse = 1.03 * (1.0 / rate_low - 1.0 / rate_high) / (2.0 * spread) + 0.5 + (rate_high - rate_low) / (6.0 * spread)
    coupling_scale = 1.0 / math.sqrt(mean_inverse)
    channel_rates = jnp.exp(jax.random.uniform(intensity_key, (1, MESH_NODES), jnp.float32, math.log(rate_low), math.log(rate_high)))
    jitter = jnp.exp(jax.random.uniform(noise_random_key, (DAY_SLOTS, MESH_NODES), jnp.float32, math.log(0.7), math.log(1.4)))
    spike_slot_list = jax.random.uniform(spike_random_key, (DAY_SLOTS, 1), jnp.float32) < 0.08
    spike_channel_list = jax.random.uniform(selection_key, (DAY_SLOTS, MESH_NODES), jnp.float32) < 0.25
    spike_layout = jnp.where(spike_slot_list & spike_channel_list, 0.6, 1.0)
    diagonal_entries = jnp.exp(-channel_rates * jitter) * spike_layout
    coupling = jax.random.normal(displacement_key, (DAY_SLOTS, MESH_NODES, MESH_NODES), jnp.float32) * (coupling_scale / math.sqrt(MESH_NODES))
    identity = jnp.eye(MESH_NODES, dtype=jnp.float32)
    return (coupling + diagonal_entries[:, :, None] * identity[None]).astype(jnp.bfloat16)


def block_levels(own_key, shape, cuts, least, largest):
    loudness = 1.0
    for dim, parts in cuts:
        draws = jax.random.uniform(jax.random.fold_in(jax.random.fold_in(own_key, 6), dim), (parts,), jnp.float32, least / len(cuts), largest / len(cuts))
        loudness = loudness * jnp.repeat(jnp.exp(draws), shape[dim] // parts).reshape((-1,) + (1,) * (len(shape) - 1 - dim))
    return loudness


def length_profile(count, total, reach, slope):
    loads = [(1 << 20) // math.isqrt(standing ** slope) + 1 for standing in range(2, count + 1)]
    rest, counts = total - reach - (count - 1), [1] * (count - 1)
    while rest > 0:
        free = [i for i in range(count - 1) if counts[i] < reach]
        pool, budget = sum([loads[i] for i in free]), rest
        for i in free:
            addition = min(reach - counts[i], max(1, budget * loads[i] // pool), rest)
            counts[i] = counts[i] + addition
            rest = rest - addition
    return np.array([reach] + counts)


def ragged(key, number_of, total, limit, slope):
    if number_of == 2:
        one = jax.random.randint(key, (), max(1, total - limit), min(limit, total - 1) + 1)
        return jnp.stack([one, total - one])
    sizes = jnp.asarray(length_profile(number_of, total, limit, slope), jnp.int32)
    pairs = (number_of - 1) // 2
    donor, receiver = sizes[1:1 + 2 * pairs:2], sizes[2:2 + 2 * pairs:2]
    room = jnp.minimum(donor - 1, limit - receiver)
    shifted = jax.random.randint(jax.random.fold_in(key, 1), (pairs,), 0, 1 << 20) % (room + 1)
    sizes = sizes.at[1:1 + 2 * pairs:2].set(donor - shifted).at[2:2 + 2 * pairs:2].set(receiver + shifted)
    return sizes[jax.random.permutation(jax.random.fold_in(key, 2), number_of)]


def bell_draw(own_key, dims, width, limit, cuts=(), held_as=jnp.bfloat16):
    level = block_levels(own_key, dims, cuts, -0.22, 0.18) if cuts else 1.0
    array = jax.random.normal(own_key, dims, jnp.float32) * width * level
    return jnp.minimum(jnp.maximum(array, -limit), limit).astype(held_as)


def setup_inputs(seed: int = 0) -> dict:
    arg_keys = jax.random.split(jax.random.key(seed), 4)
    return {
        "steps": draw_steps(jax.random.fold_in(arg_keys[3], 71), 0),
        "lengths": ragged(arg_keys[1], N_TM, 2 * N_TM, CAP, 2).astype(jnp.int32),
        "anchor": bell_draw(arg_keys[2], (MESH_NODES, COLS), 1.0, 6.0, ((1, 4),)),
    }


def reference(steps, lengths, anchor):
    slots_all = jnp.arange(DAY_SLOTS - 1, -1, -1).astype(jnp.int32)

    def advance(carry, slot):
        section = slot // CAP
        within = slot % CAP
        used = within < lengths[section]
        result = lax.cond(used, lambda: jnp.dot(steps[slot], carry, preferred_element_type=jnp.float32), lambda: jnp.zeros((MESH_NODES, COLS), jnp.float32))
        carry = jnp.where(used, result.astype(jnp.bfloat16), carry)
        return carry, result

    final, results = lax.scan(advance, anchor, slots_all)
    return results[::-1]
```

```python
import functools

import jax
import jax.numpy as jnp
from jax import lax
from jax.experimental import pallas as pl
from jax.experimental.pallas import tpu as pltpu
from jax.sharding import PartitionSpec as P

MESH = pl.DeviceIdType.MESH
CHUNK = 128
TILE = 256
SPANS = 4
GRANT = 36 << 20


def kernel(
    nt, nz, len_ref, steps_ref, anchor_ref, out_ref, full, carry, scout_out, scout_in,
    gsend, grecv, csend, crecv, ssend, srecv, asend, hsend, *spread
):
    t, z = lax.axis_index("tm"), lax.axis_index("space")
    cap, parts, share, nodes = steps_ref.shape
    rows = parts * share
    packed = bool(spread)
    width = anchor_ref.shape[1]
    chunk = min(CHUNK, width)
    tile = min(TILE, nodes)

    barrier = pltpu.get_barrier_semaphore()
    near = {"tm": range(1, nt) if packed else (1, nt - 1), "space": (1, nz - 1)}
    for axis, at, size in (("tm", t, nt), ("space", z, nz)):
        for step in near[axis]:
            pl.semaphore_signal(
                barrier,
                inc=1,
                device_id={axis: lax.rem(at + step, size)},
                device_id_type=MESH,
            )
    span = max(1, nt // SPANS)
    at_end = (z == 0) | (z == nz - 1)
    scouts = (z == 1) | (z == nz - 2)
    end = jnp.where(z <= 1, 0, nz - 1)
    scout = jnp.where(z <= 1, 1, nz - 2)
    edge = lax.rem(t, span) == 0
    gives = scouts & edge & (t > 0)
    takes = at_end & (lax.rem(t, span) == span - 1) & (t < nt - 1)

    @pl.when(gives)
    def _():
        pl.semaphore_signal(
            barrier,
            inc=1,
            device_id={"tm": t - 1, "space": end},
            device_id_type=MESH,
        )

    @pl.when(takes)
    def _():
        pl.semaphore_signal(
            barrier,
            inc=1,
            device_id={"tm": t + 1, "space": scout},
            device_id_type=MESH,
        )

    greeted = len(near["tm"]) + len(near["space"])
    pl.semaphore_wait(barrier, greeted + jnp.where(gives | takes, 1, 0))

    def stripe(k):
        return pl.ds(pl.multiple_of(k * chunk, chunk), chunk)

    def lend(k, device):
        return pltpu.make_async_remote_copy(
            src_ref=anchor_ref.at[:, stripe(k)],
            dst_ref=scout_in.at[:, stripe(k)],
            send_sem=asend.at[k],
            recv_sem=srecv.at[k],
            device_id={"space": device},
            device_id_type=MESH,
        )

    lends = at_end & (t == nt - 1)
    chunks = width // chunk

    @pl.when(lends)
    def _():
        for k in range(chunks):
            lend(k, scout).start()

    order = list(range(cap - 1, -1, -1))
    length = len_ref[0]
    pair = 2 if chunks % 2 == 0 else 1

    def block_of(slot, r):
        if tile <= share:
            part, at = divmod(r, share)
            owner, part = divmod(part, parts)
            return full[slot, owner, part, at : at + tile, :]
        if tile <= rows:
            owner, at = divmod(r, rows)
            part, count = at // share, tile // share
            return full[slot, owner, part : part + count].reshape(tile, nodes)
        return full[slot, r // rows : (r + tile) // rows].reshape(tile, nodes)

    def days(k, count, source, result, slots):
        columns = pl.ds(pl.multiple_of(k * chunk, chunk), count * chunk)
        for slot in slots:
            before = source.at[:, columns] if slot == cap - 1 else result.at[slot + 1, :, columns]
            operand = before[...]
            for r in range(0, nodes, tile):
                block = block_of(slot, r)
                value = jnp.dot(block, operand, preferred_element_type=jnp.float32)
                kept = before[r : r + tile, :].astype(jnp.float32)
                value = jnp.where(slot < length, value, kept)
                result[slot, r : r + tile, columns] = value.astype(result.dtype)

    @pl.when(t == nt - 1)
    def _():
        carry[...] = anchor_ref[...]

    def landing(s, way):
        return land[(nz - 1) * ((1 - way) // 2) + s]

    def hop(lane, s, way):
        owner = z - way * s
        d = (1 - way) // 2
        if packed and lane == 1:
            src, dst = held if s == 0 else landing(s - 1, way), landing(s, way)
        else:
            dst = full.at[lane, owner]
            src = steps_ref.at[lane] if s == 0 else dst
        return pltpu.make_async_remote_copy(
            src_ref=src,
            dst_ref=dst,
            send_sem=gsend.at[d, lane, s],
            recv_sem=grecv.at[d, lane, s],
            device_id={"space": z + way},
            device_id_type=MESH,
        )

    def sends(s, way):
        if way > 0:
            return (z >= s) & (z < nz - 1)
        return (z + s < nz) & (z > 0)

    def receives(s, way):
        return z - 1 >= s if way > 0 else z + 1 + s < nz

    def arrival(lane, s, way):
        owner = z - way * (s + 1)
        d = (1 - way) // 2
        block = landing(s, way) if packed and lane == 1 else full.at[lane, owner]
        return pltpu.make_async_remote_copy(
            src_ref=block,
            dst_ref=block,
            send_sem=gsend.at[d, lane, s],
            recv_sem=grecv.at[d, lane, s],
            device_id={"space": z - way},
            device_id_type=MESH,
        )

    def launch(slot, s):
        for way in (1, -1):

            @pl.when(sends(s, way))
            def _():
                hop(slot, s, way).start()

    def forward(lane, s):
        for way in (1, -1):

            @pl.when(receives(s, way))
            def _():
                arrival(lane, s, way).wait_recv()

            if s + 1 < nz - 1:

                @pl.when(sends(s + 1, way))
                def _():
                    hop(lane, s + 1, way).start()

    lanes = [0, 1] if packed else order
    if packed:
        note, notes, known, gift, held, mixed, lsend, lrecv, esend, erecv, dsend, drecv, *land = spread
        extra = cap - 1

        def peer(j):
            return lax.rem(t + j, nt)

        def source(j):
            return lax.rem(t + nt - j, nt)

        def tell(j, section):
            return pltpu.make_async_remote_copy(
                src_ref=note,
                dst_ref=notes.at[section],
                send_sem=lsend.at[j],
                recv_sem=lrecv.at[j],
                device_id={"tm": peer(j)},
                device_id_type=MESH,
            )

        def give(j, section):
            return pltpu.make_async_remote_copy(
                src_ref=steps_ref.at[1:cap, peer(j)],
                dst_ref=gift.at[pl.ds(section * extra, extra)],
                send_sem=esend.at[j],
                recv_sem=erecv.at[j],
                device_id={"tm": peer(j)},
                device_id_type=MESH,
            )

        def deal(j, s, way, carrier):
            d = (1 - way) // 2
            owner = z - way * (s + 1)
            return pltpu.make_async_remote_copy(
                src_ref=mixed.at[owner, peer(j)],
                dst_ref=full.at[1:cap, owner, carrier],
                send_sem=dsend.at[d, s, j],
                recv_sem=drecv.at[d, s, j],
                device_id={"tm": peer(j)},
                device_id_type=MESH,
            )

        launch(0, 0)
        note[...] = jnp.full(note.shape, len_ref[0], jnp.int32)
        for j in range(1, nt):
            tell(j, t).start()
            give(j, t).start()
        notes[t] = note[...]
        for e in range(extra):
            gift[t * extra + e] = steps_ref[1 + e, t]
        for slot in range(cap):
            full[slot, z] = steps_ref[slot]
        for j in range(1, nt):
            tell(j, source(j)).wait_recv()
        read = pltpu.make_async_copy(notes, known, lsend.at[0])
        read.start()
        read.wait()
        begin, total = [None] * nt, 0
        for section in range(nt - 1, -1, -1):
            begin[section] = total
            total = total + known[section, 0, 0] - 1
        for j in range(1, nt):
            give(j, source(j)).wait_recv()
        for k in range(nt):
            pick = 0
            for section in range(nt):
                ahead = k - begin[section]
                mine = (ahead >= 0) & (ahead < known[section, 0, 0] - 1)
                pick = jnp.where(mine, section * extra + ahead, pick)
            held[k] = gift[pick]
        launch(1, 0)
        for s in range(nz - 1):
            forward(1, s)
            forward(0, s)
            for way in (1, -1):

                @pl.when(receives(s, way))
                def _():
                    owner = z - way * (s + 1)
                    for section in range(nt):
                        for e in range(extra):
                            k = jnp.clip(begin[section] + e, 0, nt - 1)
                            mixed[owner, section, e] = landing(s, way)[k]
                    for j in range(1, nt):
                        deal(j, s, way, t).start()
                    for e in range(extra):
                        full[1 + e, owner, t] = mixed[owner, t, e]

        for s in range(nz - 1):
            for way in (1, -1):

                @pl.when(receives(s, way))
                def _():
                    for j in range(1, nt):
                        deal(j, s, way, source(j)).wait_recv()
    else:
        launch(order[0], 0)
        for i, slot in enumerate(order):
            if i + 1 < cap:
                launch(order[i + 1], 0)
            full[slot, z] = steps_ref[slot]
            for s in range(nz - 1):
                forward(slot, s)

    def pass_on(k, device):
        return pltpu.make_async_remote_copy(
            src_ref=out_ref.at[0, :, stripe(k)],
            dst_ref=carry.at[:, stripe(k)],
            send_sem=csend.at[k],
            recv_sem=crecv.at[k],
            device_id={"tm": device},
            device_id_type=MESH,
        )

    def scout_on(k, device):
        return pltpu.make_async_remote_copy(
            src_ref=scout_out.at[0, :, stripe(k)],
            dst_ref=scout_in.at[:, stripe(k)],
            send_sem=ssend.at[k],
            recv_sem=srecv.at[k],
            device_id={"tm": device},
            device_id_type=MESH,
        )

    def hand_over(k):
        return pltpu.make_async_remote_copy(
            src_ref=scout_out.at[0, :, stripe(k)],
            dst_ref=carry.at[:, stripe(k)],
            send_sem=hsend.at[k],
            recv_sem=crecv.at[k],
            device_id={"tm": t - 1, "space": end},
            device_id_type=MESH,
        )

    @pl.when(scouts & (t >= span))
    def _():
        def scout_chunk(k, _):
            scout_on(k, t - 1).wait_recv()
            days(k, 1, scout_in, scout_out, order)

            @pl.when(edge)
            def _():
                hand_over(k).start()

            @pl.when(t > span)
            def _():
                scout_on(k, t - 1).start()

            return 0

        lax.fori_loop(0, chunks, scout_chunk, 0)

    passes = (t > 0) & jnp.logical_not(at_end & edge)

    def chain(count):
        def one_chunk(j, _):
            @pl.when(t < nt - 1)
            def _():
                for k in range(count):
                    pass_on(j * count + k, t + 1).wait_recv()

            days(j * count, count, carry, out_ref, order)

            @pl.when(passes)
            def _():
                for k in range(count):
                    pass_on(j * count + k, t - 1).start()

            return 0

        lax.fori_loop(0, chunks // count, one_chunk, 0)

    @pl.when(at_end)
    def _():
        chain(pair)

    @pl.when(jnp.logical_not(at_end))
    def _():
        chain(1)

    @pl.when(lends)
    def _():
        for k in range(chunks):
            lend(k, scout).wait_send()

    @pl.when(scouts & (t > span))
    def _():
        for k in range(chunks):
            scout_on(k, t - 1).wait_send()

    @pl.when(gives)
    def _():
        for k in range(chunks):
            hand_over(k).wait_send()

    for lane in lanes:
        for s in range(nz - 1):
            for way in (1, -1):

                @pl.when(sends(s, way))
                def _():
                    hop(lane, s, way).wait_send()

    if packed:
        for j in range(1, nt):
            tell(j, t).wait_send()
            give(j, t).wait_send()
        for s in range(nz - 1):
            for way in (1, -1):

                @pl.when(receives(s, way))
                def _():
                    for j in range(1, nt):
                        deal(j, s, way, t).wait_send()

    @pl.when(passes)
    def _():
        for k in range(chunks):
            pass_on(k, t - 1).wait_send()


def shards(nt, nz, steps, lengths, anchor):
    cap, rows, nodes = steps.shape
    width = anchor.shape[1]
    packed = cap == 3 and rows % (16 * nt) == 0
    parts = nt if packed else 1
    share, extra = rows // parts, cap - 1
    steps = steps.reshape(cap, parts, share, nodes)
    spread = [
        pltpu.VMEM((8, 128), jnp.int32),
        pltpu.VMEM((nt, 8, 128), jnp.int32),
        pltpu.SMEM((nt, 8, 128), jnp.int32),
        pltpu.VMEM((nt * extra, share, nodes), jnp.bfloat16),
        pltpu.VMEM((nt, share, nodes), jnp.bfloat16),
        pltpu.VMEM((nz, nt, extra, share, nodes), jnp.bfloat16),
        pltpu.SemaphoreType.DMA((nt,)),
        pltpu.SemaphoreType.DMA((nt,)),
        pltpu.SemaphoreType.DMA((nt,)),
        pltpu.SemaphoreType.DMA((nt,)),
        pltpu.SemaphoreType.DMA((2, nz - 1, nt)),
        pltpu.SemaphoreType.DMA((2, nz - 1, nt)),
        *[pltpu.VMEM((nt, share, nodes), jnp.bfloat16)] * (2 * (nz - 1)),
    ]
    chunks = width // min(CHUNK, width)
    vmem = pl.BlockSpec(memory_space=pltpu.VMEM)
    panels = pl.pallas_call(
        functools.partial(kernel, nt, nz),
        out_shape=jax.ShapeDtypeStruct((cap, nodes, width), jnp.bfloat16),
        in_specs=[pl.BlockSpec(memory_space=pltpu.SMEM), vmem, vmem],
        out_specs=vmem,
        scratch_shapes=[
            pltpu.VMEM((cap, nz, parts, share, nodes), jnp.bfloat16),
            pltpu.VMEM((nodes, width), jnp.bfloat16),
            pltpu.VMEM((cap, nodes, width), jnp.bfloat16),
            pltpu.VMEM((nodes, width), jnp.bfloat16),
            pltpu.SemaphoreType.DMA((2, cap, nz - 1)),
            pltpu.SemaphoreType.DMA((2, cap, nz - 1)),
            pltpu.SemaphoreType.DMA((chunks,)),
            pltpu.SemaphoreType.DMA((chunks,)),
            pltpu.SemaphoreType.DMA((chunks,)),
            pltpu.SemaphoreType.DMA((chunks,)),
            pltpu.SemaphoreType.DMA((chunks,)),
            pltpu.SemaphoreType.DMA((chunks,)),
            *(spread if packed else []),
        ],
        compiler_params=pltpu.CompilerParams(
            collective_id=0, has_side_effects=True, vmem_limit_bytes=GRANT
        ),
    )(lengths, steps, anchor)
    used = jnp.arange(cap) < lengths[0]
    return jnp.where(used[:, None, None], panels.astype(jnp.float32), 0.0)


def solution(mesh):
    return jax.shard_map(
        functools.partial(shards, mesh.shape["tm"], mesh.shape["space"]),
        mesh=mesh,
        in_specs=(P("tm", "space", None), P("tm"), P(None, "space")),
        out_specs=P("tm", None, "space"),
        check_vma=False,
    )
```

```python
import functools

import jax
import jax.numpy as jnp
from jax import lax
from jax.experimental import pallas as pl
from jax.experimental.pallas import tpu as pltpu
from jax.sharding import PartitionSpec as P

MESH = pl.DeviceIdType.MESH
CHUNK = 128
TILE = 256
SPANS = 4
GRANT = 36 << 20


def kernel(
    nt, nz, len_ref, steps_ref, anchor_ref, out_ref, full, carry, scout_out, scout_in,
    gsend, grecv, csend, crecv, ssend, srecv, asend, hsend, *spread
):
    t, z = lax.axis_index("tm"), lax.axis_index("space")
    cap, parts, share, nodes = steps_ref.shape
    rows = parts * share
    packed = bool(spread)
    width = anchor_ref.shape[1]
    chunk = min(CHUNK, width)
    tile = min(TILE, nodes)

    barrier = pltpu.get_barrier_semaphore()
    near = {"tm": range(1, nt) if packed else (1, nt - 1), "space": (1, nz - 1)}
    for axis, at, size in (("tm", t, nt), ("space", z, nz)):
        for step in near[axis]:
            pl.semaphore_signal(
                barrier,
                inc=1,
                device_id={axis: lax.rem(at + step, size)},
                device_id_type=MESH,
            )
    span = max(1, nt // SPANS)
    at_end = (z == 0) | (z == nz - 1)
    scouts = (z == 1) | (z == nz - 2)
    end = jnp.where(z <= 1, 0, nz - 1)
    scout = jnp.where(z <= 1, 1, nz - 2)
    edge = lax.rem(t, span) == 0
    gives = scouts & edge & (t > 0)
    takes = at_end & (lax.rem(t, span) == span - 1) & (t < nt - 1)

    @pl.when(gives)
    def _():
        pl.semaphore_signal(
            barrier,
            inc=1,
            device_id={"tm": t - 1, "space": end},
            device_id_type=MESH,
        )

    @pl.when(takes)
    def _():
        pl.semaphore_signal(
            barrier,
            inc=1,
            device_id={"tm": t + 1, "space": scout},
            device_id_type=MESH,
        )

    greeted = len(near["tm"]) + len(near["space"])
    pl.semaphore_wait(barrier, greeted + jnp.where(gives | takes, 1, 0))

    def stripe(k):
        return pl.ds(pl.multiple_of(k * chunk, chunk), chunk)

    def lend(k, device):
        return pltpu.make_async_remote_copy(
            src_ref=anchor_ref.at[:, stripe(k)],
            dst_ref=scout_in.at[:, stripe(k)],
            send_sem=asend.at[k],
            recv_sem=srecv.at[k],
            device_id={"space": device},
            device_id_type=MESH,
        )

    lends = at_end & (t == nt - 1)
    chunks = width // chunk

    @pl.when(lends)
    def _():
        for k in range(chunks):
            lend(k, scout).start()

    order = list(range(cap - 1, -1, -1))
    length = len_ref[0]
    pair = 2 if chunks % 2 == 0 else 1

    def block_of(slot, r):
        if tile <= share:
            part, at = divmod(r, share)
            owner, part = divmod(part, parts)
            return full[slot, owner, part, at : at + tile, :]
        if tile <= rows:
            owner, at = divmod(r, rows)
            part, count = at // share, tile // share
            return full[slot, owner, part : part + count].reshape(tile, nodes)
        return full[slot, r // rows : (r + tile) // rows].reshape(tile, nodes)

    def days(k, count, source, result, slots):
        columns = pl.ds(pl.multiple_of(k * chunk, chunk), count * chunk)
        for slot in slots:
            before = source.at[:, columns] if slot == cap - 1 else result.at[slot + 1, :, columns]
            operand = before[...]
            for r in range(0, nodes, tile):
                block = block_of(slot, r)
                value = jnp.dot(block, operand, preferred_element_type=jnp.float32)
                kept = before[r : r + tile, :].astype(jnp.float32)
                value = jnp.where(slot < length, value, kept)
                result[slot, r : r + tile, columns] = value.astype(result.dtype)

    @pl.when(t == nt - 1)
    def _():
        carry[...] = anchor_ref[...]

    def hop(slot, s, way):
        owner = z - way * s
        d = (1 - way) // 2
        block = full.at[slot, owner]
        return pltpu.make_async_remote_copy(
            src_ref=steps_ref.at[slot] if s == 0 else block,
            dst_ref=block,
            send_sem=gsend.at[d, slot, s],
            recv_sem=grecv.at[d, slot, s],
            device_id={"space": z + way},
            device_id_type=MESH,
        )

    def sends(s, way):
        if way > 0:
            return (z >= s) & (z < nz - 1)
        return (z + s < nz) & (z > 0)

    def receives(s, way):
        return z - 1 >= s if way > 0 else z + 1 + s < nz

    def arrival(slot, s, way):
        owner = z - way * (s + 1)
        d = (1 - way) // 2
        block = full.at[slot, owner]
        return pltpu.make_async_remote_copy(
            src_ref=block,
            dst_ref=block,
            send_sem=gsend.at[d, slot, s],
            recv_sem=grecv.at[d, slot, s],
            device_id={"space": z - way},
            device_id_type=MESH,
        )

    def launch(slot, s):
        for way in (1, -1):

            @pl.when(sends(s, way))
            def _():
                hop(slot, s, way).start()

    def forward(lane, s):
        for way in (1, -1):

            @pl.when(receives(s, way))
            def _():
                arrival(lane, s, way).wait_recv()

            if s + 1 < nz - 1:

                @pl.when(sends(s + 1, way))
                def _():
                    hop(lane, s + 1, way).start()

    lanes = [0] if packed else order
    if packed:
        note, notes, known, held, mixed, lsend, lrecv, esend, erecv, dsend, drecv, hsends, hrecvs = spread[:13]
        pieces = held.shape[0]
        gift, land = spread[13 : 13 + pieces], spread[13 + pieces :]
        piece = share // pieces
        extra = cap - 1

        def peer(j):
            return lax.rem(t + j, nt)

        def source(j):
            return lax.rem(t + nt - j, nt)

        def tell(j, section):
            return pltpu.make_async_remote_copy(
                src_ref=note,
                dst_ref=notes.at[section],
                send_sem=lsend.at[j],
                recv_sem=lrecv.at[j],
                device_id={"tm": peer(j)},
                device_id_type=MESH,
            )

        def give(j, p, section):
            return pltpu.make_async_remote_copy(
                src_ref=steps_ref.at[1:cap, peer(j), p * piece : (p + 1) * piece],
                dst_ref=gift[p].at[pl.ds(section * extra, extra)],
                send_sem=esend.at[p, j],
                recv_sem=erecv.at[p, j],
                device_id={"tm": peer(j)},
                device_id_type=MESH,
            )

        def landing(p, s, way):
            return land[((1 - way) // 2 * (nz - 1) + s) * pieces + p]

        def carry_on(p, s, way):
            d = (1 - way) // 2
            return pltpu.make_async_remote_copy(
                src_ref=held.at[p] if s == 0 else landing(p, s - 1, way),
                dst_ref=landing(p, s, way),
                send_sem=hsends.at[d, p, s],
                recv_sem=hrecvs.at[d, p, s],
                device_id={"space": z + way},
                device_id_type=MESH,
            )

        def lands(p, s, way):
            d = (1 - way) // 2
            return pltpu.make_async_remote_copy(
                src_ref=landing(p, s, way),
                dst_ref=landing(p, s, way),
                send_sem=hsends.at[d, p, s],
                recv_sem=hrecvs.at[d, p, s],
                device_id={"space": z - way},
                device_id_type=MESH,
            )

        def deal(j, p, s, way, carrier):
            d = (1 - way) // 2
            owner = z - way * (s + 1)
            return pltpu.make_async_remote_copy(
                src_ref=mixed.at[p, owner, peer(j)],
                dst_ref=full.at[1:cap, owner, carrier, p * piece : (p + 1) * piece],
                send_sem=dsend.at[d, p, s, j],
                recv_sem=drecv.at[d, p, s, j],
                device_id={"tm": peer(j)},
                device_id_type=MESH,
            )

        launch(0, 0)
        note[...] = jnp.full(note.shape, len_ref[0], jnp.int32)
        for j in range(1, nt):
            tell(j, t).start()
        for p in range(pieces):
            for j in range(1, nt):
                give(j, p, t).start()
        notes[t] = note[...]
        for p in range(pieces):
            for e in range(extra):
                gift[p][t * extra + e] = steps_ref[1 + e, t, p * piece : (p + 1) * piece]
        for j in range(1, nt):
            tell(j, source(j)).wait_recv()
        read = pltpu.make_async_copy(notes, known, lsend.at[0])
        read.start()
        read.wait()
        begin, total = [None] * nt, 0
        for section in range(nt - 1, -1, -1):
            begin[section] = total
            total = total + known[section, 0, 0] - 1
        picks = []
        for k in range(nt):
            pick = 0
            for section in range(nt):
                ahead = k - begin[section]
                mine = (ahead >= 0) & (ahead < known[section, 0, 0] - 1)
                pick = jnp.where(mine, section * extra + ahead, pick)
            picks.append(pick)
        for p in range(pieces):
            for j in range(1, nt):
                give(j, p, source(j)).wait_recv()
            for k in range(nt):
                held[p, k] = gift[p][picks[k]]
            for way in (1, -1):

                @pl.when(sends(0, way))
                def _():
                    carry_on(p, 0, way).start()

        for slot in range(cap):
            full[slot, z] = steps_ref[slot]
        for s in range(nz - 1):
            for p in range(pieces):
                for way in (1, -1):

                    @pl.when(receives(s, way))
                    def _():
                        lands(p, s, way).wait_recv()

                    if s + 1 < nz - 1:

                        @pl.when(sends(s + 1, way))
                        def _():
                            carry_on(p, s + 1, way).start()

                    @pl.when(receives(s, way))
                    def _():
                        owner = z - way * (s + 1)
                        for section in range(nt):
                            for e in range(extra):
                                k = jnp.clip(begin[section] + e, 0, nt - 1)
                                mixed[p, owner, section, e] = landing(p, s, way)[k]
                        for j in range(1, nt):
                            deal(j, p, s, way, t).start()
                        for e in range(extra):
                            full[1 + e, owner, t, p * piece : (p + 1) * piece] = mixed[p, owner, t, e]

        for s in range(nz - 1):
            forward(0, s)
        for s in range(nz - 1):
            for way in (1, -1):

                @pl.when(receives(s, way))
                def _():
                    for p in range(pieces):
                        for j in range(1, nt):
                            deal(j, p, s, way, source(j)).wait_recv()
    else:
        launch(order[0], 0)
        for i, slot in enumerate(order):
            if i + 1 < cap:
                launch(order[i + 1], 0)
            full[slot, z] = steps_ref[slot]
            for s in range(nz - 1):
                forward(slot, s)

    def pass_on(k, device):
        return pltpu.make_async_remote_copy(
            src_ref=out_ref.at[0, :, stripe(k)],
            dst_ref=carry.at[:, stripe(k)],
            send_sem=csend.at[k],
            recv_sem=crecv.at[k],
            device_id={"tm": device},
            device_id_type=MESH,
        )

    def scout_on(k, device):
        return pltpu.make_async_remote_copy(
            src_ref=scout_out.at[0, :, stripe(k)],
            dst_ref=scout_in.at[:, stripe(k)],
            send_sem=ssend.at[k],
            recv_sem=srecv.at[k],
            device_id={"tm": device},
            device_id_type=MESH,
        )

    def hand_over(k):
        return pltpu.make_async_remote_copy(
            src_ref=scout_out.at[0, :, stripe(k)],
            dst_ref=carry.at[:, stripe(k)],
            send_sem=hsend.at[k],
            recv_sem=crecv.at[k],
            device_id={"tm": t - 1, "space": end},
            device_id_type=MESH,
        )

    @pl.when(scouts & (t >= span))
    def _():
        def scout_chunk(k, _):
            scout_on(k, t - 1).wait_recv()
            days(k, 1, scout_in, scout_out, order)

            @pl.when(edge)
            def _():
                hand_over(k).start()

            @pl.when(t > span)
            def _():
                scout_on(k, t - 1).start()

            return 0

        lax.fori_loop(0, chunks, scout_chunk, 0)

    passes = (t > 0) & jnp.logical_not(at_end & edge)

    def chain(count):
        def one_chunk(j, _):
            @pl.when(t < nt - 1)
            def _():
                for k in range(count):
                    pass_on(j * count + k, t + 1).wait_recv()

            days(j * count, count, carry, out_ref, order)

            @pl.when(passes)
            def _():
                for k in range(count):
                    pass_on(j * count + k, t - 1).start()

            return 0

        lax.fori_loop(0, chunks // count, one_chunk, 0)

    @pl.when(at_end)
    def _():
        chain(pair)

    @pl.when(jnp.logical_not(at_end))
    def _():
        chain(1)

    @pl.when(lends)
    def _():
        for k in range(chunks):
            lend(k, scout).wait_send()

    @pl.when(scouts & (t > span))
    def _():
        for k in range(chunks):
            scout_on(k, t - 1).wait_send()

    @pl.when(gives)
    def _():
        for k in range(chunks):
            hand_over(k).wait_send()

    for lane in lanes:
        for s in range(nz - 1):
            for way in (1, -1):

                @pl.when(sends(s, way))
                def _():
                    hop(lane, s, way).wait_send()

    if packed:
        for j in range(1, nt):
            tell(j, t).wait_send()
            for p in range(pieces):
                give(j, p, t).wait_send()
        for s in range(nz - 1):
            for way in (1, -1):
                for p in range(pieces):

                    @pl.when(sends(s, way))
                    def _():
                        carry_on(p, s, way).wait_send()

                    @pl.when(receives(s, way))
                    def _():
                        for j in range(1, nt):
                            deal(j, p, s, way, t).wait_send()

    @pl.when(passes)
    def _():
        for k in range(chunks):
            pass_on(k, t - 1).wait_send()


def shards(nt, nz, steps, lengths, anchor):
    cap, rows, nodes = steps.shape
    width = anchor.shape[1]
    packed = cap == 3 and rows % (16 * nt) == 0
    parts = nt if packed else 1
    share, extra = rows // parts, cap - 1
    steps = steps.reshape(cap, parts, share, nodes)
    pieces = 2 if share % 32 == 0 else 1
    piece = share // pieces
    vmem16 = lambda *shape: pltpu.VMEM(shape, jnp.bfloat16)
    dma = pltpu.SemaphoreType.DMA
    spread = [
        pltpu.VMEM((8, 128), jnp.int32),
        pltpu.VMEM((nt, 8, 128), jnp.int32),
        pltpu.SMEM((nt, 8, 128), jnp.int32),
        vmem16(pieces, nt, piece, nodes),
        vmem16(pieces, nz, nt, extra, piece, nodes),
        dma((nt,)),
        dma((nt,)),
        dma((pieces, nt)),
        dma((pieces, nt)),
        dma((2, pieces, nz - 1, nt)),
        dma((2, pieces, nz - 1, nt)),
        dma((2, pieces, nz - 1)),
        dma((2, pieces, nz - 1)),
        *[vmem16(nt * extra, piece, nodes)] * pieces,
        *[vmem16(nt, piece, nodes)] * (2 * (nz - 1) * pieces),
    ]
    chunks = width // min(CHUNK, width)
    vmem = pl.BlockSpec(memory_space=pltpu.VMEM)
    panels = pl.pallas_call(
        functools.partial(kernel, nt, nz),
        out_shape=jax.ShapeDtypeStruct((cap, nodes, width), jnp.bfloat16),
        in_specs=[pl.BlockSpec(memory_space=pltpu.SMEM), vmem, vmem],
        out_specs=vmem,
        scratch_shapes=[
            pltpu.VMEM((cap, nz, parts, share, nodes), jnp.bfloat16),
            pltpu.VMEM((nodes, width), jnp.bfloat16),
            pltpu.VMEM((cap, nodes, width), jnp.bfloat16),
            pltpu.VMEM((nodes, width), jnp.bfloat16),
            pltpu.SemaphoreType.DMA((2, cap, nz - 1)),
            pltpu.SemaphoreType.DMA((2, cap, nz - 1)),
            pltpu.SemaphoreType.DMA((chunks,)),
            pltpu.SemaphoreType.DMA((chunks,)),
            pltpu.SemaphoreType.DMA((chunks,)),
            pltpu.SemaphoreType.DMA((chunks,)),
            pltpu.SemaphoreType.DMA((chunks,)),
            pltpu.SemaphoreType.DMA((chunks,)),
            *(spread if packed else []),
        ],
        compiler_params=pltpu.CompilerParams(
            collective_id=0, has_side_effects=True, vmem_limit_bytes=GRANT
        ),
    )(lengths, steps, anchor)
    used = jnp.arange(cap) < lengths[0]
    return jnp.where(used[:, None, None], panels.astype(jnp.float32), 0.0)


def solution(mesh):
    return jax.shard_map(
        functools.partial(shards, mesh.shape["tm"], mesh.shape["space"]),
        mesh=mesh,
        in_specs=(P("tm", "space", None), P("tm"), P(None, "space")),
        out_specs=P("tm", None, "space"),
        check_vma=False,
    )
```

```python
import functools

import jax
import jax.numpy as jnp
from jax import lax
from jax.experimental import pallas as pl
from jax.experimental.pallas import tpu as pltpu
from jax.sharding import PartitionSpec as P

MESH = pl.DeviceIdType.MESH
CHUNK = 128
TILE = 256
SPANS = 4
PARTS = 2
GRANT = 36 << 20


def kernel(
    nt, nz, len_ref, steps_ref, anchor_ref, out_ref, full, carry, scout_out, scout_in,
    total, gsend, grecv, csend, crecv, ssend, srecv, asend, hsend, *spread
):
    t, z = lax.axis_index("tm"), lax.axis_index("space")
    cap, parts, share, nodes = steps_ref.shape
    rows = parts * share
    packed = bool(spread)
    width = anchor_ref.shape[1]
    chunk = min(CHUNK, width)
    tile = min(TILE, nodes)

    barrier = pltpu.get_barrier_semaphore()
    near = {"tm": range(1, nt) if packed else (1, nt - 1), "space": (1, nz - 1)}
    for axis, at, size in (("tm", t, nt), ("space", z, nz)):
        for step in near[axis]:
            pl.semaphore_signal(
                barrier,
                inc=1,
                device_id={axis: lax.rem(at + step, size)},
                device_id_type=MESH,
            )
    span = max(1, nt // SPANS)
    at_end = (z == 0) | (z == nz - 1)
    scouts = (z == 1) | (z == nz - 2)
    end = jnp.where(z <= 1, 0, nz - 1)
    scout = jnp.where(z <= 1, 1, nz - 2)
    edge = lax.rem(t, span) == 0
    crossed = edge & (t > 0) & (t < nt - span)
    gives = scouts & crossed
    takes = at_end & (lax.rem(t, span) == span - 1) & (t < nt - 1 - span)

    @pl.when(gives)
    def _():
        pl.semaphore_signal(
            barrier,
            inc=1,
            device_id={"tm": t - 1, "space": end},
            device_id_type=MESH,
        )

    @pl.when(takes)
    def _():
        pl.semaphore_signal(
            barrier,
            inc=1,
            device_id={"tm": t + 1, "space": scout},
            device_id_type=MESH,
        )

    greeted = len(near["tm"]) + len(near["space"])
    pl.semaphore_wait(barrier, greeted + jnp.where(gives | takes, 1, 0))

    def stripe(k):
        return pl.ds(pl.multiple_of(k * chunk, chunk), chunk)

    half = nodes // PARTS

    def strip(q):
        return pl.ds(q * half, half)

    def lend(k, q, device):
        return pltpu.make_async_remote_copy(
            src_ref=anchor_ref.at[strip(q), stripe(k)],
            dst_ref=scout_in.at[strip(q), stripe(k)],
            send_sem=asend.at[k, q],
            recv_sem=srecv.at[k, q],
            device_id={"space": device},
            device_id_type=MESH,
        )

    lends = at_end & (t == nt - 1)
    chunks = width // chunk

    scouted = (chunks + 1) // 2

    @pl.when(lends)
    def _():
        for k in range(scouted):
            for q in range(PARTS):
                lend(k, q, scout).start()

    order = list(range(cap - 1, -1, -1))
    length = len_ref[0]

    def block_of(slot, r, cols):
        if tile <= share:
            part, at = divmod(r, share)
            owner, part = divmod(part, parts)
            return full[slot, owner, part, at : at + tile, cols]
        if tile <= rows:
            owner, at = divmod(r, rows)
            part, count = at // share, tile // share
            block = full[slot, owner, part : part + count, :, cols]
        else:
            block = full[slot, r // rows : (r + tile) // rows, :, :, cols]
        return block.reshape(tile, block.shape[-1])

    def days(k, source, result, arrive, depart):
        columns = stripe(k)
        for slot in order:
            before = source.at[:, columns] if slot == cap - 1 else result.at[slot + 1, :, columns]
            stages = PARTS if slot == cap - 1 else 1
            depth = nodes // stages
            for q in range(stages):
                if slot == cap - 1:
                    arrive(q)
                span_q = slice(q * depth, (q + 1) * depth)
                operand = before[span_q, :]
                for r in range(0, nodes, tile):
                    value = jnp.dot(
                        block_of(slot, r, span_q), operand, preferred_element_type=jnp.float32
                    )
                    if q > 0:
                        value = total[r : r + tile, :] + value
                    if q < stages - 1:
                        total[r : r + tile, :] = value
                        continue
                    kept = before[r : r + tile, :].astype(jnp.float32)
                    value = jnp.where(slot < length, value, kept)
                    result[slot, r : r + tile, columns] = value.astype(result.dtype)
                    if slot == 0 and (r + tile) % half == 0:
                        depart(r // half)

    @pl.when(t == nt - 1)
    def _():
        carry[...] = anchor_ref[...]

    def hop(slot, s, way):
        owner = z - way * s
        d = (1 - way) // 2
        block = full.at[slot, owner]
        return pltpu.make_async_remote_copy(
            src_ref=steps_ref.at[slot] if s == 0 else block,
            dst_ref=block,
            send_sem=gsend.at[d, slot, s],
            recv_sem=grecv.at[d, slot, s],
            device_id={"space": z + way},
            device_id_type=MESH,
        )

    def sends(s, way):
        if way > 0:
            return (z >= s) & (z < nz - 1)
        return (z + s < nz) & (z > 0)

    def receives(s, way):
        return z - 1 >= s if way > 0 else z + 1 + s < nz

    def arrival(slot, s, way):
        owner = z - way * (s + 1)
        d = (1 - way) // 2
        block = full.at[slot, owner]
        return pltpu.make_async_remote_copy(
            src_ref=block,
            dst_ref=block,
            send_sem=gsend.at[d, slot, s],
            recv_sem=grecv.at[d, slot, s],
            device_id={"space": z - way},
            device_id_type=MESH,
        )

    def launch(slot, s):
        for way in (-1, 1):

            @pl.when(sends(s, way))
            def _():
                hop(slot, s, way).start()

    def forward(lane, s):
        for way in (-1, 1):

            @pl.when(receives(s, way))
            def _():
                arrival(lane, s, way).wait_recv()

            if s + 1 < nz - 1:

                @pl.when(sends(s + 1, way))
                def _():
                    hop(lane, s + 1, way).start()

    lanes = [0] if packed else order
    if packed:
        note, notes, known, held, mixed, lsend, lrecv, esend, erecv, dsend, drecv, hsends, hrecvs = spread[:13]
        pieces = held.shape[0]
        gift, land = spread[13 : 13 + pieces], spread[13 + pieces :]
        piece = share // pieces
        extra = cap - 1

        def peer(j):
            return lax.rem(t + j, nt)

        def source(j):
            return lax.rem(t + nt - j, nt)

        def tell(j, section):
            return pltpu.make_async_remote_copy(
                src_ref=note,
                dst_ref=notes.at[section],
                send_sem=lsend.at[j],
                recv_sem=lrecv.at[j],
                device_id={"tm": peer(j)},
                device_id_type=MESH,
            )

        def give(j, p, section):
            return pltpu.make_async_remote_copy(
                src_ref=steps_ref.at[1:cap, peer(j), p * piece : (p + 1) * piece],
                dst_ref=gift[p].at[pl.ds(section * extra, extra)],
                send_sem=esend.at[p, j],
                recv_sem=erecv.at[p, j],
                device_id={"tm": peer(j)},
                device_id_type=MESH,
            )

        def landing(p, s, way):
            return land[((1 - way) // 2 * (nz - 1) + s) * pieces + p]

        def carry_on(p, s, way):
            d = (1 - way) // 2
            return pltpu.make_async_remote_copy(
                src_ref=held.at[p] if s == 0 else landing(p, s - 1, way),
                dst_ref=landing(p, s, way),
                send_sem=hsends.at[d, p, s],
                recv_sem=hrecvs.at[d, p, s],
                device_id={"space": z + way},
                device_id_type=MESH,
            )

        def lands(p, s, way):
            d = (1 - way) // 2
            return pltpu.make_async_remote_copy(
                src_ref=landing(p, s, way),
                dst_ref=landing(p, s, way),
                send_sem=hsends.at[d, p, s],
                recv_sem=hrecvs.at[d, p, s],
                device_id={"space": z - way},
                device_id_type=MESH,
            )

        def deal(j, p, s, way, carrier):
            d = (1 - way) // 2
            owner = z - way * (s + 1)
            return pltpu.make_async_remote_copy(
                src_ref=mixed.at[p, owner, peer(j)],
                dst_ref=full.at[1:cap, owner, carrier, p * piece : (p + 1) * piece],
                send_sem=dsend.at[d, p, s, j],
                recv_sem=drecv.at[d, p, s, j],
                device_id={"tm": peer(j)},
                device_id_type=MESH,
            )

        launch(0, 0)
        note[...] = jnp.full(note.shape, len_ref[0], jnp.int32)
        for j in range(1, nt):
            tell(j, t).start()
        for p in range(pieces):
            for j in range(1, nt):
                give(j, p, t).start()
        notes[t] = note[...]
        for p in range(pieces):
            for e in range(extra):
                gift[p][t * extra + e] = steps_ref[1 + e, t, p * piece : (p + 1) * piece]
        for j in range(1, nt):
            tell(j, source(j)).wait_recv()
        read = pltpu.make_async_copy(notes, known, lsend.at[0])
        read.start()
        read.wait()
        begin, ahead = [None] * nt, 0
        for section in range(nt - 1, -1, -1):
            begin[section] = ahead
            ahead = ahead + known[section, 0, 0] - 1
        picks = []
        for k in range(nt):
            pick = 0
            for section in range(nt):
                ahead = k - begin[section]
                mine = (ahead >= 0) & (ahead < known[section, 0, 0] - 1)
                pick = jnp.where(mine, section * extra + ahead, pick)
            picks.append(pick)
        for p in range(pieces):
            for j in range(1, nt):
                give(j, p, source(j)).wait_recv()
            for k in range(nt):
                held[p, k] = gift[p][picks[k]]
            for way in (-1, 1):

                @pl.when(sends(0, way))
                def _():
                    carry_on(p, 0, way).start()

        for slot in range(cap):
            full[slot, z] = steps_ref[slot]
        for s in range(nz - 1):
            for p in range(pieces):
                for way in (-1, 1):

                    @pl.when(receives(s, way))
                    def _():
                        lands(p, s, way).wait_recv()

                    if s + 1 < nz - 1:

                        @pl.when(sends(s + 1, way))
                        def _():
                            carry_on(p, s + 1, way).start()

                for way in (-1, 1):

                    @pl.when(receives(s, way))
                    def _():
                        owner = z - way * (s + 1)
                        for section in range(nt):
                            for e in range(extra):
                                k = jnp.clip(begin[section] + e, 0, nt - 1)
                                mixed[p, owner, section, e] = landing(p, s, way)[k]
                        for j in range(1, nt):
                            deal(j, p, s, way, t).start()
                        for e in range(extra):
                            full[1 + e, owner, t, p * piece : (p + 1) * piece] = mixed[p, owner, t, e]

            forward(0, s)

        for s in range(nz - 1):
            for way in (-1, 1):

                @pl.when(receives(s, way))
                def _():
                    for p in range(pieces):
                        for j in range(1, nt):
                            deal(j, p, s, way, source(j)).wait_recv()
    else:
        launch(order[0], 0)
        for i, slot in enumerate(order):
            if i + 1 < cap:
                launch(order[i + 1], 0)
            full[slot, z] = steps_ref[slot]
            for s in range(nz - 1):
                forward(slot, s)

    def pass_on(k, q, device):
        return pltpu.make_async_remote_copy(
            src_ref=out_ref.at[0, strip(q), stripe(k)],
            dst_ref=carry.at[strip(q), stripe(k)],
            send_sem=csend.at[k, q],
            recv_sem=crecv.at[k, q],
            device_id={"tm": device},
            device_id_type=MESH,
        )

    def scout_on(k, q, device):
        return pltpu.make_async_remote_copy(
            src_ref=scout_out.at[0, strip(q), stripe(k)],
            dst_ref=scout_in.at[strip(q), stripe(k)],
            send_sem=ssend.at[k, q],
            recv_sem=srecv.at[k, q],
            device_id={"tm": device},
            device_id_type=MESH,
        )

    def hand_over(k, q):
        return pltpu.make_async_remote_copy(
            src_ref=scout_out.at[0, strip(q), stripe(k)],
            dst_ref=carry.at[strip(q), stripe(k)],
            send_sem=hsend.at[k, q],
            recv_sem=crecv.at[k, q],
            device_id={"tm": t - 1, "space": end},
            device_id_type=MESH,
        )

    @pl.when(scouts & (t >= span))
    def _():
        def scout_chunk(k, _):
            def arrive(q):
                scout_on(k, q, t - 1).wait_recv()

            def depart(q):
                @pl.when(crossed)
                def _():
                    hand_over(k, q).start()

                @pl.when(t > span)
                def _():
                    scout_on(k, q, t - 1).start()

            days(k, scout_in, scout_out, arrive, depart)
            return 0

        lax.fori_loop(0, scouted, scout_chunk, 0)

    given = at_end & crossed
    turn = jnp.where(at_end & (t >= nt - 2 * span), scouted, 0)

    def one_chunk(j, _):
        k = lax.rem(j + turn, chunks)

        def arrive(q):
            @pl.when(t < nt - 1)
            def _():
                pass_on(k, q, t + 1).wait_recv()

        def depart(q):
            @pl.when((t > 0) & jnp.logical_not(given & (k < scouted)))
            def _():
                pass_on(k, q, t - 1).start()

        days(k, carry, out_ref, arrive, depart)
        return 0

    lax.fori_loop(0, chunks, one_chunk, 0)

    @pl.when(lends)
    def _():
        for k in range(scouted):
            for q in range(PARTS):
                lend(k, q, scout).wait_send()

    @pl.when(scouts & (t > span))
    def _():
        for k in range(scouted):
            for q in range(PARTS):
                scout_on(k, q, t - 1).wait_send()

    @pl.when(gives)
    def _():
        for k in range(scouted):
            for q in range(PARTS):
                hand_over(k, q).wait_send()

    for lane in lanes:
        for s in range(nz - 1):
            for way in (-1, 1):

                @pl.when(sends(s, way))
                def _():
                    hop(lane, s, way).wait_send()

    if packed:
        for j in range(1, nt):
            tell(j, t).wait_send()
            for p in range(pieces):
                give(j, p, t).wait_send()
        for s in range(nz - 1):
            for way in (-1, 1):
                for p in range(pieces):

                    @pl.when(sends(s, way))
                    def _():
                        carry_on(p, s, way).wait_send()

                    @pl.when(receives(s, way))
                    def _():
                        for j in range(1, nt):
                            deal(j, p, s, way, t).wait_send()

    for k in range(chunks):
        kept = given if k < scouted else False

        @pl.when((t > 0) & jnp.logical_not(kept))
        def _():
            for q in range(PARTS):
                pass_on(k, q, t - 1).wait_send()


def shards(nt, nz, steps, lengths, anchor):
    cap, rows, nodes = steps.shape
    width = anchor.shape[1]
    packed = cap == 3 and rows % (16 * nt) == 0
    parts = nt if packed else 1
    share, extra = rows // parts, cap - 1
    steps = steps.reshape(cap, parts, share, nodes)
    pieces = 2 if share % 32 == 0 else 1
    piece = share // pieces
    vmem16 = lambda *shape: pltpu.VMEM(shape, jnp.bfloat16)
    dma = pltpu.SemaphoreType.DMA
    spread = [
        pltpu.VMEM((8, 128), jnp.int32),
        pltpu.VMEM((nt, 8, 128), jnp.int32),
        pltpu.SMEM((nt, 8, 128), jnp.int32),
        vmem16(pieces, nt, piece, nodes),
        vmem16(pieces, nz, nt, extra, piece, nodes),
        dma((nt,)),
        dma((nt,)),
        dma((pieces, nt)),
        dma((pieces, nt)),
        dma((2, pieces, nz - 1, nt)),
        dma((2, pieces, nz - 1, nt)),
        dma((2, pieces, nz - 1)),
        dma((2, pieces, nz - 1)),
        *[vmem16(nt * extra, piece, nodes)] * pieces,
        *[vmem16(nt, piece, nodes)] * (2 * (nz - 1) * pieces),
    ]
    chunks = width // min(CHUNK, width)
    vmem = pl.BlockSpec(memory_space=pltpu.VMEM)
    panels = pl.pallas_call(
        functools.partial(kernel, nt, nz),
        out_shape=jax.ShapeDtypeStruct((cap, nodes, width), jnp.bfloat16),
        in_specs=[pl.BlockSpec(memory_space=pltpu.SMEM), vmem, vmem],
        out_specs=vmem,
        scratch_shapes=[
            pltpu.VMEM((cap, nz, parts, share, nodes), jnp.bfloat16),
            pltpu.VMEM((nodes, width), jnp.bfloat16),
            pltpu.VMEM((cap, nodes, width), jnp.bfloat16),
            pltpu.VMEM((nodes, width), jnp.bfloat16),
            pltpu.VMEM((nodes, min(CHUNK, width)), jnp.float32),
            pltpu.SemaphoreType.DMA((2, cap, nz - 1)),
            pltpu.SemaphoreType.DMA((2, cap, nz - 1)),
            pltpu.SemaphoreType.DMA((chunks, PARTS)),
            pltpu.SemaphoreType.DMA((chunks, PARTS)),
            pltpu.SemaphoreType.DMA((chunks, PARTS)),
            pltpu.SemaphoreType.DMA((chunks, PARTS)),
            pltpu.SemaphoreType.DMA((chunks, PARTS)),
            pltpu.SemaphoreType.DMA((chunks, PARTS)),
            *(spread if packed else []),
        ],
        compiler_params=pltpu.CompilerParams(
            collective_id=0, has_side_effects=True, vmem_limit_bytes=GRANT
        ),
    )(lengths, steps, anchor)
    used = jnp.arange(cap) < lengths[0]
    return jnp.where(used[:, None, None], panels.astype(jnp.float32), 0.0)


def solution(mesh):
    return jax.shard_map(
        functools.partial(shards, mesh.shape["tm"], mesh.shape["space"]),
        mesh=mesh,
        in_specs=(P("tm", "space", None), P("tm"), P(None, "space")),
        out_specs=P("tm", None, "space"),
        check_vma=False,
    )
```

```python
import functools

import jax
import jax.numpy as jnp
from jax import lax
from jax.experimental import pallas as pl
from jax.experimental.pallas import tpu as pltpu
from jax.sharding import PartitionSpec as P

MESH = pl.DeviceIdType.MESH
CHUNK = 128
TILE = 256
SPANS = 4
PARTS = 2
EVEN = (6, 7, 2, 5, 3, 4, 1)
ODD = (6, 7, 4, 3, 5, 2, 1)
GRANT = 36 << 20


def kernel(
    nt, nz, len_ref, steps_ref, anchor_ref, out_ref, full, carry, scout_out, scout_in,
    total, gsend, grecv, csend, crecv, ssend, srecv, asend, hsend, *spread
):
    t, z = lax.axis_index("tm"), lax.axis_index("space")
    cap, parts, share, nodes = steps_ref.shape
    rows = parts * share
    packed = bool(spread)
    width = anchor_ref.shape[1]
    chunk = min(CHUNK, width)
    tile = min(TILE, nodes)

    barrier = pltpu.get_barrier_semaphore()
    near = {"tm": range(1, nt) if packed else (1, nt - 1), "space": (1, nz - 1)}
    for axis, at, size in (("tm", t, nt), ("space", z, nz)):
        for step in near[axis]:
            pl.semaphore_signal(
                barrier,
                inc=1,
                device_id={axis: lax.rem(at + step, size)},
                device_id_type=MESH,
            )
    span = max(1, nt // SPANS)
    at_end = (z == 0) | (z == nz - 1)
    scouts = (z == 1) | (z == nz - 2)
    end = jnp.where(z <= 1, 0, nz - 1)
    scout = jnp.where(z <= 1, 1, nz - 2)
    edge = lax.rem(t, span) == 0
    crossed = edge & (t > 0) & (t < nt - span)
    gives = scouts & crossed
    takes = at_end & (lax.rem(t, span) == span - 1) & (t < nt - 1 - span)

    @pl.when(gives)
    def _():
        pl.semaphore_signal(
            barrier,
            inc=1,
            device_id={"tm": t - 1, "space": end},
            device_id_type=MESH,
        )

    @pl.when(takes)
    def _():
        pl.semaphore_signal(
            barrier,
            inc=1,
            device_id={"tm": t + 1, "space": scout},
            device_id_type=MESH,
        )

    greeted = len(near["tm"]) + len(near["space"])
    pl.semaphore_wait(barrier, greeted + jnp.where(gives | takes, 1, 0))

    def stripe(k):
        return pl.ds(pl.multiple_of(k * chunk, chunk), chunk)

    half = nodes // PARTS

    def strip(q):
        return pl.ds(q * half, half)

    def lend(k, q, device):
        return pltpu.make_async_remote_copy(
            src_ref=anchor_ref.at[strip(q), stripe(k)],
            dst_ref=scout_in.at[strip(q), stripe(k)],
            send_sem=asend.at[k, q],
            recv_sem=srecv.at[k, q],
            device_id={"space": device},
            device_id_type=MESH,
        )

    lends = at_end & (t == nt - 1)
    chunks = width // chunk

    scouted = (3 * chunks + 3) // 4

    @pl.when(lends)
    def _():
        for k in range(scouted):
            for q in range(PARTS):
                lend(k, q, scout).start()

    order = list(range(cap - 1, -1, -1))
    length = len_ref[0]

    def block_of(slot, r, cols):
        if tile <= share:
            part, at = divmod(r, share)
            owner, part = divmod(part, parts)
            return full[slot, owner, part, at : at + tile, cols]
        if tile <= rows:
            owner, at = divmod(r, rows)
            part, count = at // share, tile // share
            block = full[slot, owner, part : part + count, :, cols]
        else:
            block = full[slot, r // rows : (r + tile) // rows, :, :, cols]
        return block.reshape(tile, block.shape[-1])

    def days(k, source, result, arrive, depart):
        columns = stripe(k)
        for slot in order:
            before = source.at[:, columns] if slot == cap - 1 else result.at[slot + 1, :, columns]
            stages = PARTS if slot == cap - 1 else 1
            depth = nodes // stages
            for q in range(stages):
                if slot == cap - 1:
                    arrive(q)
                span_q = slice(q * depth, (q + 1) * depth)
                operand = before[span_q, :]
                for r in range(0, nodes, tile):
                    value = jnp.dot(
                        block_of(slot, r, span_q), operand, preferred_element_type=jnp.float32
                    )
                    if q > 0:
                        value = total[r : r + tile, :] + value
                    if q < stages - 1:
                        total[r : r + tile, :] = value
                        continue
                    kept = before[r : r + tile, :].astype(jnp.float32)
                    value = jnp.where(slot < length, value, kept)
                    result[slot, r : r + tile, columns] = value.astype(result.dtype)
                    if slot == 0 and (r + tile) % half == 0:
                        depart(r // half)

    @pl.when(t == nt - 1)
    def _():
        carry[...] = anchor_ref[...]

    def hop(slot, s, way):
        owner = z - way * s
        d = (1 - way) // 2
        block = full.at[slot, owner]
        return pltpu.make_async_remote_copy(
            src_ref=steps_ref.at[slot] if s == 0 else block,
            dst_ref=block,
            send_sem=gsend.at[d, slot, s],
            recv_sem=grecv.at[d, slot, s],
            device_id={"space": z + way},
            device_id_type=MESH,
        )

    def sends(s, way):
        if way > 0:
            return (z >= s) & (z < nz - 1)
        return (z + s < nz) & (z > 0)

    def receives(s, way):
        return z - 1 >= s if way > 0 else z + 1 + s < nz

    def arrival(slot, s, way):
        owner = z - way * (s + 1)
        d = (1 - way) // 2
        block = full.at[slot, owner]
        return pltpu.make_async_remote_copy(
            src_ref=block,
            dst_ref=block,
            send_sem=gsend.at[d, slot, s],
            recv_sem=grecv.at[d, slot, s],
            device_id={"space": z - way},
            device_id_type=MESH,
        )

    def launch(slot, s):
        for way in (-1, 1):

            @pl.when(sends(s, way))
            def _():
                hop(slot, s, way).start()

    def forward(lane, s):
        for way in (-1, 1):

            @pl.when(receives(s, way))
            def _():
                arrival(lane, s, way).wait_recv()

            if s + 1 < nz - 1:

                @pl.when(sends(s + 1, way))
                def _():
                    hop(lane, s + 1, way).start()

    lanes = [0] if packed else order
    if packed:
        note, notes, known, held, mixed, lsend, lrecv, esend, erecv, dsend, drecv, hsends, hrecvs = spread[:13]
        pieces = held.shape[0]
        gift, land = spread[13 : 13 + pieces], spread[13 + pieces :]
        piece = share // pieces
        extra = cap - 1

        def link(j):
            if nt != 8:
                return j
            return jnp.where(lax.rem(t, 2) == 0, EVEN[j - 1], ODD[j - 1])

        def peer(j):
            if nt != 8:
                return lax.rem(t + j, nt)
            device, bit = 0, 1
            while bit < nt:
                mine, other = lax.rem(t // bit, 2), lax.rem(link(j) // bit, 2)
                device = device + bit * (mine + other - 2 * mine * other)
                bit *= 2
            return device

        def source(j):
            return lax.rem(t + nt - j, nt) if nt != 8 else peer(j)

        def tell(j, section):
            return pltpu.make_async_remote_copy(
                src_ref=note,
                dst_ref=notes.at[section],
                send_sem=lsend.at[link(j)],
                recv_sem=lrecv.at[link(j)],
                device_id={"tm": peer(j)},
                device_id_type=MESH,
            )

        def give(j, p, section):
            return pltpu.make_async_remote_copy(
                src_ref=steps_ref.at[1:cap, peer(j), p * piece : (p + 1) * piece],
                dst_ref=gift[p].at[pl.ds(section * extra, extra)],
                send_sem=esend.at[p, link(j)],
                recv_sem=erecv.at[p, link(j)],
                device_id={"tm": peer(j)},
                device_id_type=MESH,
            )

        def landing(p, s, way):
            return land[((1 - way) // 2 * (nz - 1) + s) * pieces + p]

        def carry_on(p, s, way):
            d = (1 - way) // 2
            return pltpu.make_async_remote_copy(
                src_ref=held.at[p] if s == 0 else landing(p, s - 1, way),
                dst_ref=landing(p, s, way),
                send_sem=hsends.at[d, p, s],
                recv_sem=hrecvs.at[d, p, s],
                device_id={"space": z + way},
                device_id_type=MESH,
            )

        def lands(p, s, way):
            d = (1 - way) // 2
            return pltpu.make_async_remote_copy(
                src_ref=landing(p, s, way),
                dst_ref=landing(p, s, way),
                send_sem=hsends.at[d, p, s],
                recv_sem=hrecvs.at[d, p, s],
                device_id={"space": z - way},
                device_id_type=MESH,
            )

        def deal(j, p, s, way, carrier):
            d = (1 - way) // 2
            owner = z - way * (s + 1)
            return pltpu.make_async_remote_copy(
                src_ref=mixed.at[p, owner, peer(j)],
                dst_ref=full.at[1:cap, owner, carrier, p * piece : (p + 1) * piece],
                send_sem=dsend.at[d, p, s, link(j)],
                recv_sem=drecv.at[d, p, s, link(j)],
                device_id={"tm": peer(j)},
                device_id_type=MESH,
            )

        launch(0, 0)
        note[...] = jnp.full(note.shape, len_ref[0], jnp.int32)
        for j in range(1, nt):
            tell(j, t).start()
        for p in range(pieces):
            for j in range(1, nt):
                give(j, p, t).start()
        notes[t] = note[...]
        for p in range(pieces):
            for e in range(extra):
                gift[p][t * extra + e] = steps_ref[1 + e, t, p * piece : (p + 1) * piece]
        for j in range(1, nt):
            tell(j, source(j)).wait_recv()
        read = pltpu.make_async_copy(notes, known, lsend.at[0])
        read.start()
        read.wait()
        begin, ahead = [None] * nt, 0
        for section in range(nt - 1, -1, -1):
            begin[section] = ahead
            ahead = ahead + known[section, 0, 0] - 1
        picks = []
        for k in range(nt):
            pick = 0
            for section in range(nt):
                ahead = k - begin[section]
                mine = (ahead >= 0) & (ahead < known[section, 0, 0] - 1)
                pick = jnp.where(mine, section * extra + ahead, pick)
            picks.append(pick)
        for p in range(pieces):
            for j in range(1, nt):
                give(j, p, source(j)).wait_recv()
            for k in range(nt):
                held[p, k] = gift[p][picks[k]]
            for way in (-1, 1):

                @pl.when(sends(0, way))
                def _():
                    carry_on(p, 0, way).start()

        for slot in range(cap):
            full[slot, z] = steps_ref[slot]
        for s in range(nz - 1):
            for p in range(pieces):
                for way in (-1, 1):

                    @pl.when(receives(s, way))
                    def _():
                        lands(p, s, way).wait_recv()

                    if s + 1 < nz - 1:

                        @pl.when(sends(s + 1, way))
                        def _():
                            carry_on(p, s + 1, way).start()

                for way in (-1, 1):

                    @pl.when(receives(s, way))
                    def _():
                        owner = z - way * (s + 1)
                        for section in range(nt):
                            for e in range(extra):
                                k = jnp.clip(begin[section] + e, 0, nt - 1)
                                mixed[p, owner, section, e] = landing(p, s, way)[k]
                        for j in range(1, nt):
                            deal(j, p, s, way, t).start()
                        for e in range(extra):
                            full[1 + e, owner, t, p * piece : (p + 1) * piece] = mixed[p, owner, t, e]

            forward(0, s)

        for s in range(nz - 1):
            for way in (-1, 1):

                @pl.when(receives(s, way))
                def _():
                    for p in range(pieces):
                        for j in range(1, nt):
                            deal(j, p, s, way, source(j)).wait_recv()
    else:
        launch(order[0], 0)
        for i, slot in enumerate(order):
            if i + 1 < cap:
                launch(order[i + 1], 0)
            full[slot, z] = steps_ref[slot]
            for s in range(nz - 1):
                forward(slot, s)

    def pass_on(k, q, device):
        return pltpu.make_async_remote_copy(
            src_ref=out_ref.at[0, strip(q), stripe(k)],
            dst_ref=carry.at[strip(q), stripe(k)],
            send_sem=csend.at[k, q],
            recv_sem=crecv.at[k, q],
            device_id={"tm": device},
            device_id_type=MESH,
        )

    def scout_on(k, q, device):
        return pltpu.make_async_remote_copy(
            src_ref=scout_out.at[0, strip(q), stripe(k)],
            dst_ref=scout_in.at[strip(q), stripe(k)],
            send_sem=ssend.at[k, q],
            recv_sem=srecv.at[k, q],
            device_id={"tm": device},
            device_id_type=MESH,
        )

    def hand_over(k, q):
        return pltpu.make_async_remote_copy(
            src_ref=scout_out.at[0, strip(q), stripe(k)],
            dst_ref=carry.at[strip(q), stripe(k)],
            send_sem=hsend.at[k, q],
            recv_sem=crecv.at[k, q],
            device_id={"tm": t - 1, "space": end},
            device_id_type=MESH,
        )

    @pl.when(scouts & (t >= span))
    def _():
        def scout_chunk(k, _):
            def arrive(q):
                scout_on(k, q, t - 1).wait_recv()

            def depart(q):
                @pl.when(crossed)
                def _():
                    hand_over(k, q).start()

                @pl.when(t > span)
                def _():
                    scout_on(k, q, t - 1).start()

            days(k, scout_in, scout_out, arrive, depart)
            return 0

        lax.fori_loop(0, scouted, scout_chunk, 0)

    given = at_end & crossed
    turn = jnp.where(at_end & (t >= nt - 2 * span), scouted, 0)

    def one_chunk(j, _):
        k = lax.rem(j + turn, chunks)

        def arrive(q):
            @pl.when(t < nt - 1)
            def _():
                pass_on(k, q, t + 1).wait_recv()

        def depart(q):
            @pl.when((t > 0) & jnp.logical_not(given & (k < scouted)))
            def _():
                pass_on(k, q, t - 1).start()

        days(k, carry, out_ref, arrive, depart)
        return 0

    lax.fori_loop(0, chunks, one_chunk, 0)

    @pl.when(lends)
    def _():
        for k in range(scouted):
            for q in range(PARTS):
                lend(k, q, scout).wait_send()

    @pl.when(scouts & (t > span))
    def _():
        for k in range(scouted):
            for q in range(PARTS):
                scout_on(k, q, t - 1).wait_send()

    @pl.when(gives)
    def _():
        for k in range(scouted):
            for q in range(PARTS):
                hand_over(k, q).wait_send()

    for lane in lanes:
        for s in range(nz - 1):
            for way in (-1, 1):

                @pl.when(sends(s, way))
                def _():
                    hop(lane, s, way).wait_send()

    if packed:
        for j in range(1, nt):
            tell(j, t).wait_send()
            for p in range(pieces):
                give(j, p, t).wait_send()
        for s in range(nz - 1):
            for way in (-1, 1):
                for p in range(pieces):

                    @pl.when(sends(s, way))
                    def _():
                        carry_on(p, s, way).wait_send()

                    @pl.when(receives(s, way))
                    def _():
                        for j in range(1, nt):
                            deal(j, p, s, way, t).wait_send()

    for k in range(chunks):
        kept = given if k < scouted else False

        @pl.when((t > 0) & jnp.logical_not(kept))
        def _():
            for q in range(PARTS):
                pass_on(k, q, t - 1).wait_send()


def shards(nt, nz, steps, lengths, anchor):
    cap, rows, nodes = steps.shape
    width = anchor.shape[1]
    packed = cap == 3 and rows % (16 * nt) == 0
    parts = nt if packed else 1
    share, extra = rows // parts, cap - 1
    steps = steps.reshape(cap, parts, share, nodes)
    pieces = 2 if share % 32 == 0 else 1
    piece = share // pieces
    vmem16 = lambda *shape: pltpu.VMEM(shape, jnp.bfloat16)
    dma = pltpu.SemaphoreType.DMA
    spread = [
        pltpu.VMEM((8, 128), jnp.int32),
        pltpu.VMEM((nt, 8, 128), jnp.int32),
        pltpu.SMEM((nt, 8, 128), jnp.int32),
        vmem16(pieces, nt, piece, nodes),
        vmem16(pieces, nz, nt, extra, piece, nodes),
        dma((nt,)),
        dma((nt,)),
        dma((pieces, nt)),
        dma((pieces, nt)),
        dma((2, pieces, nz - 1, nt)),
        dma((2, pieces, nz - 1, nt)),
        dma((2, pieces, nz - 1)),
        dma((2, pieces, nz - 1)),
        *[vmem16(nt * extra, piece, nodes)] * pieces,
        *[vmem16(nt, piece, nodes)] * (2 * (nz - 1) * pieces),
    ]
    chunks = width // min(CHUNK, width)
    vmem = pl.BlockSpec(memory_space=pltpu.VMEM)
    panels = pl.pallas_call(
        functools.partial(kernel, nt, nz),
        out_shape=jax.ShapeDtypeStruct((cap, nodes, width), jnp.bfloat16),
        in_specs=[pl.BlockSpec(memory_space=pltpu.SMEM), vmem, vmem],
        out_specs=vmem,
        scratch_shapes=[
            pltpu.VMEM((cap, nz, parts, share, nodes), jnp.bfloat16),
            pltpu.VMEM((nodes, width), jnp.bfloat16),
            pltpu.VMEM((cap, nodes, width), jnp.bfloat16),
            pltpu.VMEM((nodes, width), jnp.bfloat16),
            pltpu.VMEM((nodes, min(CHUNK, width)), jnp.float32),
            pltpu.SemaphoreType.DMA((2, cap, nz - 1)),
            pltpu.SemaphoreType.DMA((2, cap, nz - 1)),
            pltpu.SemaphoreType.DMA((chunks, PARTS)),
            pltpu.SemaphoreType.DMA((chunks, PARTS)),
            pltpu.SemaphoreType.DMA((chunks, PARTS)),
            pltpu.SemaphoreType.DMA((chunks, PARTS)),
            pltpu.SemaphoreType.DMA((chunks, PARTS)),
            pltpu.SemaphoreType.DMA((chunks, PARTS)),
            *(spread if packed else []),
        ],
        compiler_params=pltpu.CompilerParams(
            collective_id=0, has_side_effects=True, vmem_limit_bytes=GRANT
        ),
    )(lengths, steps, anchor)
    used = jnp.arange(cap) < lengths[0]
    return jnp.where(used[:, None, None], panels.astype(jnp.float32), 0.0)


def solution(mesh):
    return jax.shard_map(
        functools.partial(shards, mesh.shape["tm"], mesh.shape["space"]),
        mesh=mesh,
        in_specs=(P("tm", "space", None), P("tm"), P(None, "space")),
        out_specs=P("tm", None, "space"),
        check_vma=False,
    )
```

```python
import functools

import jax
import jax.numpy as jnp
from jax import lax
from jax.experimental import pallas as pl
from jax.experimental.pallas import tpu as pltpu
from jax.sharding import PartitionSpec as P

MESH = pl.DeviceIdType.MESH
CHUNK = 128
TILE = 256
SPANS = 4
PARTS = 2
EVEN = (6, 7, 2, 5, 3, 4, 1)
ODD = (6, 7, 4, 3, 5, 2, 1)
GRANT = 36 << 20


def kernel(
    nt, nz, len_ref, steps_ref, anchor_ref, out_ref, full, carry, scout_out, scout_in,
    total, gsend, grecv, csend, crecv, ssend, srecv, asend, hsend, *spread
):
    t, z = lax.axis_index("tm"), lax.axis_index("space")
    cap, parts, share, nodes = steps_ref.shape
    rows = parts * share
    packed = bool(spread)
    width = anchor_ref.shape[1]
    chunk = min(CHUNK, width)
    tile = min(TILE, nodes)

    barrier = pltpu.get_barrier_semaphore()
    near = {"tm": range(1, nt) if packed else (1, nt - 1), "space": (1, nz - 1)}
    for axis, at, size in (("tm", t, nt), ("space", z, nz)):
        for step in near[axis]:
            pl.semaphore_signal(
                barrier,
                inc=1,
                device_id={axis: lax.rem(at + step, size)},
                device_id_type=MESH,
            )
    span = max(1, nt // SPANS)
    at_end = (z == 0) | (z == nz - 1)
    scouts = (z == 1) | (z == nz - 2)
    end = jnp.where(z <= 1, 0, nz - 1)
    scout = jnp.where(z <= 1, 1, nz - 2)
    edge = lax.rem(t, span) == 0
    crossed = edge & (t > 0) & (t < nt - span)
    gives = scouts & crossed
    takes = at_end & (lax.rem(t, span) == span - 1) & (t < nt - 1 - span)

    @pl.when(gives)
    def _():
        pl.semaphore_signal(
            barrier,
            inc=1,
            device_id={"tm": t - 1, "space": end},
            device_id_type=MESH,
        )

    @pl.when(takes)
    def _():
        pl.semaphore_signal(
            barrier,
            inc=1,
            device_id={"tm": t + 1, "space": scout},
            device_id_type=MESH,
        )

    greeted = len(near["tm"]) + len(near["space"])
    pl.semaphore_wait(barrier, greeted + jnp.where(gives | takes, 1, 0))

    def stripe(k):
        return pl.ds(pl.multiple_of(k * chunk, chunk), chunk)

    half = nodes // PARTS

    def strip(q):
        return pl.ds(q * half, half)

    def lend(k, q, device):
        return pltpu.make_async_remote_copy(
            src_ref=anchor_ref.at[strip(q), stripe(k)],
            dst_ref=scout_in.at[strip(q), stripe(k)],
            send_sem=asend.at[k, q],
            recv_sem=srecv.at[k, q],
            device_id={"space": device},
            device_id_type=MESH,
        )

    lends = at_end & (t == nt - 1)
    chunks = width // chunk

    scouted = (3 * chunks + 3) // 4

    @pl.when(lends)
    def _():
        for k in range(scouted):
            for q in range(PARTS):
                lend(k, q, scout).start()

    order = list(range(cap - 1, -1, -1))
    length = len_ref[0]

    def block_of(slot, r, cols):
        if tile <= share:
            part, at = divmod(r, share)
            owner, part = divmod(part, parts)
            return full[slot, owner, part, at : at + tile, cols]
        if tile <= rows:
            owner, at = divmod(r, rows)
            part, count = at // share, tile // share
            block = full[slot, owner, part : part + count, :, cols]
        else:
            block = full[slot, r // rows : (r + tile) // rows, :, :, cols]
        return block.reshape(tile, block.shape[-1])

    def days(k, source, result, arrive, depart):
        columns = stripe(k)
        for slot in order:
            before = source.at[:, columns] if slot == cap - 1 else result.at[slot + 1, :, columns]
            stages = PARTS if slot == cap - 1 else 1
            depth = nodes // stages
            for q in range(stages):
                if slot == cap - 1:
                    arrive(q)
                span_q = slice(q * depth, (q + 1) * depth)
                operand = before[span_q, :]
                for r in range(0, nodes, tile):
                    value = jnp.dot(
                        block_of(slot, r, span_q), operand, preferred_element_type=jnp.float32
                    )
                    if q > 0:
                        value = total[r : r + tile, :] + value
                    if q < stages - 1:
                        total[r : r + tile, :] = value
                        continue
                    kept = before[r : r + tile, :].astype(jnp.float32)
                    value = jnp.where(slot < length, value, kept)
                    result[slot, r : r + tile, columns] = value.astype(result.dtype)
                    if slot == 0 and (r + tile) % half == 0:
                        depart(r // half)

    @pl.when(t == nt - 1)
    def _():
        carry[...] = anchor_ref[...]

    def hop(slot, s, way):
        owner = z - way * s
        d = (1 - way) // 2
        block = full.at[slot, owner]
        return pltpu.make_async_remote_copy(
            src_ref=steps_ref.at[slot] if s == 0 else block,
            dst_ref=block,
            send_sem=gsend.at[d, slot, s],
            recv_sem=grecv.at[d, slot, s],
            device_id={"space": z + way},
            device_id_type=MESH,
        )

    def sends(s, way):
        if way > 0:
            return (z >= s) & (z < nz - 1)
        return (z + s < nz) & (z > 0)

    def receives(s, way):
        return z - 1 >= s if way > 0 else z + 1 + s < nz

    def arrival(slot, s, way):
        owner = z - way * (s + 1)
        d = (1 - way) // 2
        block = full.at[slot, owner]
        return pltpu.make_async_remote_copy(
            src_ref=block,
            dst_ref=block,
            send_sem=gsend.at[d, slot, s],
            recv_sem=grecv.at[d, slot, s],
            device_id={"space": z - way},
            device_id_type=MESH,
        )

    def launch(slot, s):
        for way in (-1, 1):

            @pl.when(sends(s, way))
            def _():
                hop(slot, s, way).start()

    def forward(lane, s):
        for way in (-1, 1):

            @pl.when(receives(s, way))
            def _():
                arrival(lane, s, way).wait_recv()

            if s + 1 < nz - 1:

                @pl.when(sends(s + 1, way))
                def _():
                    hop(lane, s + 1, way).start()

    lanes = [0] if packed else order
    if packed:
        note, notes, known, held, mixed, lsend, lrecv, esend, erecv, dsend, drecv, hsends, hrecvs = spread[:13]
        pieces = held.shape[0]
        gift, land = spread[13 : 13 + pieces], spread[13 + pieces :]
        piece = share // pieces
        extra = cap - 1

        def link(j):
            if nt != 8:
                return j
            return jnp.where(lax.rem(t, 2) == 0, EVEN[j - 1], ODD[j - 1])

        def peer(j):
            if nt != 8:
                return lax.rem(t + j, nt)
            device, bit = 0, 1
            while bit < nt:
                mine, other = lax.rem(t // bit, 2), lax.rem(link(j) // bit, 2)
                device = device + bit * (mine + other - 2 * mine * other)
                bit *= 2
            return device

        def source(j):
            return lax.rem(t + nt - j, nt) if nt != 8 else peer(j)

        def tell(j, section):
            return pltpu.make_async_remote_copy(
                src_ref=note,
                dst_ref=notes.at[section],
                send_sem=lsend.at[link(j)],
                recv_sem=lrecv.at[link(j)],
                device_id={"tm": peer(j)},
                device_id_type=MESH,
            )

        def give(j, p, section):
            return pltpu.make_async_remote_copy(
                src_ref=steps_ref.at[1:cap, peer(j), p * piece : (p + 1) * piece],
                dst_ref=gift[p].at[pl.ds(section * extra, extra)],
                send_sem=esend.at[p, link(j)],
                recv_sem=erecv.at[p, link(j)],
                device_id={"tm": peer(j)},
                device_id_type=MESH,
            )

        def landing(p, s, way):
            return land[((1 - way) // 2 * (nz - 1) + s) * pieces + p]

        def carry_on(p, s, way):
            d = (1 - way) // 2
            return pltpu.make_async_remote_copy(
                src_ref=held.at[p] if s == 0 else landing(p, s - 1, way),
                dst_ref=landing(p, s, way),
                send_sem=hsends.at[d, p, s],
                recv_sem=hrecvs.at[d, p, s],
                device_id={"space": z + way},
                device_id_type=MESH,
            )

        def lands(p, s, way):
            d = (1 - way) // 2
            return pltpu.make_async_remote_copy(
                src_ref=landing(p, s, way),
                dst_ref=landing(p, s, way),
                send_sem=hsends.at[d, p, s],
                recv_sem=hrecvs.at[d, p, s],
                device_id={"space": z - way},
                device_id_type=MESH,
            )

        def deal(j, p, s, way, carrier):
            d = (1 - way) // 2
            owner = z - way * (s + 1)
            return pltpu.make_async_remote_copy(
                src_ref=mixed.at[p, owner, peer(j)],
                dst_ref=full.at[1:cap, owner, carrier, p * piece : (p + 1) * piece],
                send_sem=dsend.at[d, p, s, link(j)],
                recv_sem=drecv.at[d, p, s, link(j)],
                device_id={"tm": peer(j)},
                device_id_type=MESH,
            )

        launch(0, 0)
        note[...] = jnp.full(note.shape, len_ref[0], jnp.int32)
        for j in range(1, nt):
            tell(j, t).start()
        for p in range(pieces):
            for j in range(1, nt):
                give(j, p, t).start()
        notes[t] = note[...]
        for p in range(pieces):
            for e in range(extra):
                gift[p][t * extra + e] = steps_ref[1 + e, t, p * piece : (p + 1) * piece]
        for j in range(1, nt):
            tell(j, source(j)).wait_recv()
        read = pltpu.make_async_copy(notes, known, lsend.at[0])
        read.start()
        read.wait()
        begin, ahead = [None] * nt, 0
        for section in range(nt - 1, -1, -1):
            begin[section] = ahead
            ahead = ahead + known[section, 0, 0] - 1
        picks = []
        for k in range(nt):
            pick = 0
            for section in range(nt):
                ahead = k - begin[section]
                mine = (ahead >= 0) & (ahead < known[section, 0, 0] - 1)
                pick = jnp.where(mine, section * extra + ahead, pick)
            picks.append(pick)
        for p in range(pieces):
            for j in range(1, nt):
                give(j, p, source(j)).wait_recv()
            for k in range(nt):
                held[p, k] = gift[p][picks[k]]
            for way in (-1, 1):

                @pl.when(sends(0, way))
                def _():
                    carry_on(p, 0, way).start()

        for slot in range(cap):
            full[slot, z] = steps_ref[slot]
        for s in range(nz - 1):
            for p in range(pieces):
                for way in (-1, 1):

                    @pl.when(receives(s, way))
                    def _():
                        lands(p, s, way).wait_recv()

                    if s + 1 < nz - 1:

                        @pl.when(sends(s + 1, way))
                        def _():
                            carry_on(p, s + 1, way).start()

                for way in (-1, 1):

                    @pl.when(receives(s, way))
                    def _():
                        owner = z - way * (s + 1)
                        for section in range(nt):
                            for e in range(extra):
                                k = jnp.clip(begin[section] + e, 0, nt - 1)
                                mixed[p, owner, section, e] = landing(p, s, way)[k]
                        for j in range(1, nt):
                            deal(j, p, s, way, t).start()
                        for e in range(extra):
                            full[1 + e, owner, t, p * piece : (p + 1) * piece] = mixed[p, owner, t, e]

            forward(0, s)

        for s in range(nz - 1):
            for way in (-1, 1):

                @pl.when(receives(s, way))
                def _():
                    for p in range(pieces):
                        for j in range(1, nt):
                            deal(j, p, s, way, source(j)).wait_recv()
    else:
        launch(order[0], 0)
        for i, slot in enumerate(order):
            if i + 1 < cap:
                launch(order[i + 1], 0)
            full[slot, z] = steps_ref[slot]
            for s in range(nz - 1):
                forward(slot, s)

    def pass_on(k, q, device):
        return pltpu.make_async_remote_copy(
            src_ref=out_ref.at[0, strip(q), stripe(k)],
            dst_ref=carry.at[strip(q), stripe(k)],
            send_sem=csend.at[k, q],
            recv_sem=crecv.at[k, q],
            device_id={"tm": device},
            device_id_type=MESH,
        )

    def scout_on(k, q, device):
        return pltpu.make_async_remote_copy(
            src_ref=scout_out.at[0, strip(q), stripe(k)],
            dst_ref=scout_in.at[strip(q), stripe(k)],
            send_sem=ssend.at[k, q],
            recv_sem=srecv.at[k, q],
            device_id={"tm": device},
            device_id_type=MESH,
        )

    def hand_over(k, q):
        return pltpu.make_async_remote_copy(
            src_ref=scout_out.at[0, strip(q), stripe(k)],
            dst_ref=carry.at[strip(q), stripe(k)],
            send_sem=hsend.at[k, q],
            recv_sem=crecv.at[k, q],
            device_id={"tm": t - 1, "space": end},
            device_id_type=MESH,
        )

    @pl.when(scouts & (t >= span))
    def _():
        def scout_chunk(k, _):
            def arrive(q):
                scout_on(k, q, t - 1).wait_recv()

            def depart(q):
                @pl.when(crossed)
                def _():
                    hand_over(k, q).start()

                @pl.when(t > span)
                def _():
                    scout_on(k, q, t - 1).start()

            days(k, scout_in, scout_out, arrive, depart)
            return 0

        lax.fori_loop(0, scouted, scout_chunk, 0)

    given = at_end & crossed
    turn = jnp.where(at_end & (t >= nt - 2 * span), scouted, 0)

    def one_chunk(j, _):
        k = lax.rem(j + turn, chunks)

        def arrive(q):
            @pl.when(t < nt - 1)
            def _():
                pass_on(k, q, t + 1).wait_recv()

        def depart(q):
            @pl.when((t > 0) & jnp.logical_not(given & (k < scouted)))
            def _():
                pass_on(k, q, t - 1).start()

        days(k, carry, out_ref, arrive, depart)
        return 0

    lax.fori_loop(0, chunks, one_chunk, 0)

    @pl.when(lends)
    def _():
        for k in range(scouted):
            for q in range(PARTS):
                lend(k, q, scout).wait_send()

    @pl.when(scouts & (t > span))
    def _():
        for k in range(scouted):
            for q in range(PARTS):
                scout_on(k, q, t - 1).wait_send()

    @pl.when(gives)
    def _():
        for k in range(scouted):
            for q in range(PARTS):
                hand_over(k, q).wait_send()

    for lane in lanes:
        for s in range(nz - 1):
            for way in (-1, 1):

                @pl.when(sends(s, way))
                def _():
                    hop(lane, s, way).wait_send()

    if packed:
        for j in range(1, nt):
            tell(j, t).wait_send()
            for p in range(pieces):
                give(j, p, t).wait_send()
        for s in range(nz - 1):
            for way in (-1, 1):
                for p in range(pieces):

                    @pl.when(sends(s, way))
                    def _():
                        carry_on(p, s, way).wait_send()

                    @pl.when(receives(s, way))
                    def _():
                        for j in range(1, nt):
                            deal(j, p, s, way, t).wait_send()

    for k in range(chunks):
        kept = given if k < scouted else False

        @pl.when((t > 0) & jnp.logical_not(kept))
        def _():
            for q in range(PARTS):
                pass_on(k, q, t - 1).wait_send()


def widen(len_ref, panels_ref, out_ref, wide, sems):
    cap, nodes, _ = panels_ref.shape
    depth = min(TILE, nodes)
    copies = []
    for slot in range(cap):
        for i, r in enumerate(range(0, nodes, depth)):
            rows = pl.ds(r, depth)
            value = panels_ref[slot, rows, :].astype(jnp.float32)
            wide[slot, rows, :] = jnp.where(slot < len_ref[0], value, 0.0)
            copy = pltpu.make_async_copy(
                wide.at[slot, rows], out_ref.at[slot, rows], sems.at[slot, i]
            )
            copy.start()
            copies.append(copy)
    for copy in copies:
        copy.wait()


def shards(nt, nz, steps, lengths, anchor):
    cap, rows, nodes = steps.shape
    width = anchor.shape[1]
    packed = cap == 3 and rows % (16 * nt) == 0
    parts = nt if packed else 1
    share, extra = rows // parts, cap - 1
    steps = steps.reshape(cap, parts, share, nodes)
    pieces = 2 if share % 32 == 0 else 1
    piece = share // pieces
    vmem16 = lambda *shape: pltpu.VMEM(shape, jnp.bfloat16)
    dma = pltpu.SemaphoreType.DMA
    spread = [
        pltpu.VMEM((8, 128), jnp.int32),
        pltpu.VMEM((nt, 8, 128), jnp.int32),
        pltpu.SMEM((nt, 8, 128), jnp.int32),
        vmem16(pieces, nt, piece, nodes),
        vmem16(pieces, nz, nt, extra, piece, nodes),
        dma((nt,)),
        dma((nt,)),
        dma((pieces, nt)),
        dma((pieces, nt)),
        dma((2, pieces, nz - 1, nt)),
        dma((2, pieces, nz - 1, nt)),
        dma((2, pieces, nz - 1)),
        dma((2, pieces, nz - 1)),
        *[vmem16(nt * extra, piece, nodes)] * pieces,
        *[vmem16(nt, piece, nodes)] * (2 * (nz - 1) * pieces),
    ]
    chunks = width // min(CHUNK, width)
    vmem = pl.BlockSpec(memory_space=pltpu.VMEM)
    panels = pl.pallas_call(
        functools.partial(kernel, nt, nz),
        out_shape=jax.ShapeDtypeStruct((cap, nodes, width), jnp.bfloat16),
        in_specs=[pl.BlockSpec(memory_space=pltpu.SMEM), vmem, vmem],
        out_specs=vmem,
        scratch_shapes=[
            pltpu.VMEM((cap, nz, parts, share, nodes), jnp.bfloat16),
            pltpu.VMEM((nodes, width), jnp.bfloat16),
            pltpu.VMEM((cap, nodes, width), jnp.bfloat16),
            pltpu.VMEM((nodes, width), jnp.bfloat16),
            pltpu.VMEM((nodes, min(CHUNK, width)), jnp.float32),
            pltpu.SemaphoreType.DMA((2, cap, nz - 1)),
            pltpu.SemaphoreType.DMA((2, cap, nz - 1)),
            pltpu.SemaphoreType.DMA((chunks, PARTS)),
            pltpu.SemaphoreType.DMA((chunks, PARTS)),
            pltpu.SemaphoreType.DMA((chunks, PARTS)),
            pltpu.SemaphoreType.DMA((chunks, PARTS)),
            pltpu.SemaphoreType.DMA((chunks, PARTS)),
            pltpu.SemaphoreType.DMA((chunks, PARTS)),
            *(spread if packed else []),
        ],
        compiler_params=pltpu.CompilerParams(
            collective_id=0, has_side_effects=True, vmem_limit_bytes=GRANT
        ),
    )(lengths, steps, anchor)
    shape = (cap, nodes, width)
    return pl.pallas_call(
        widen,
        out_shape=jax.ShapeDtypeStruct(shape, jnp.float32),
        in_specs=[pl.BlockSpec(memory_space=pltpu.SMEM), vmem],
        out_specs=pl.BlockSpec(memory_space=pl.ANY),
        scratch_shapes=[
            pltpu.VMEM(shape, jnp.float32),
            pltpu.SemaphoreType.DMA((cap, nodes // min(TILE, nodes))),
        ],
        compiler_params=pltpu.CompilerParams(vmem_limit_bytes=GRANT),
    )(lengths, panels)


def solution(mesh):
    return jax.shard_map(
        functools.partial(shards, mesh.shape["tm"], mesh.shape["space"]),
        mesh=mesh,
        in_specs=(P("tm", "space", None), P("tm"), P(None, "space")),
        out_specs=P("tm", None, "space"),
        check_vma=False,
    )
```

```python
import functools

import jax
import jax.numpy as jnp
from jax import lax
from jax.experimental import pallas as pl
from jax.experimental.pallas import tpu as pltpu
from jax.sharding import PartitionSpec as P

MESH = pl.DeviceIdType.MESH
CHUNK = 128
TILE = 256
SPANS = 4
PARTS = 2
EVEN = (6, 7, 2, 5, 3, 4, 1)
ODD = (6, 7, 4, 3, 5, 2, 1)
GRANT = 60 << 20


def kernel(
    nt, nz, len_ref, steps_far, anchor_far, out_far, out_ref, stores, steps_ref, anchor_ref, loads, full, carry, scout_out, scout_in,
    total, gsend, grecv, csend, crecv, ssend, srecv, asend, hsend, *spread
):
    t, z = lax.axis_index("tm"), lax.axis_index("space")
    cap, parts, share, nodes = steps_ref.shape
    rows = parts * share
    packed = bool(spread)
    width = anchor_ref.shape[1]
    chunk = min(CHUNK, width)
    tile = min(TILE, nodes)

    fetches = [
        pltpu.make_async_copy(steps_far, steps_ref, loads.at[0]),
        pltpu.make_async_copy(anchor_far, anchor_ref, loads.at[1]),
    ]
    for fetch in fetches:
        fetch.start()

    barrier = pltpu.get_barrier_semaphore()
    near = {"tm": range(1, nt) if packed else (1, nt - 1), "space": (1, nz - 1)}
    for axis, at, size in (("tm", t, nt), ("space", z, nz)):
        for step in near[axis]:
            pl.semaphore_signal(
                barrier,
                inc=1,
                device_id={axis: lax.rem(at + step, size)},
                device_id_type=MESH,
            )
    span = max(1, nt // SPANS)
    at_end = (z == 0) | (z == nz - 1)
    scouts = (z == 1) | (z == nz - 2)
    end = jnp.where(z <= 1, 0, nz - 1)
    scout = jnp.where(z <= 1, 1, nz - 2)
    edge = lax.rem(t, span) == 0
    crossed = edge & (t > 0) & (t < nt - span)
    gives = scouts & crossed
    takes = at_end & (lax.rem(t, span) == span - 1) & (t < nt - 1 - span)

    @pl.when(gives)
    def _():
        pl.semaphore_signal(
            barrier,
            inc=1,
            device_id={"tm": t - 1, "space": end},
            device_id_type=MESH,
        )

    @pl.when(takes)
    def _():
        pl.semaphore_signal(
            barrier,
            inc=1,
            device_id={"tm": t + 1, "space": scout},
            device_id_type=MESH,
        )

    greeted = len(near["tm"]) + len(near["space"])
    pl.semaphore_wait(barrier, greeted + jnp.where(gives | takes, 1, 0))
    for fetch in fetches:
        fetch.wait()

    def stripe(k):
        return pl.ds(pl.multiple_of(k * chunk, chunk), chunk)

    half = nodes // PARTS

    def strip(q):
        return pl.ds(q * half, half)

    def lend(k, q, device):
        return pltpu.make_async_remote_copy(
            src_ref=anchor_ref.at[strip(q), stripe(k)],
            dst_ref=scout_in.at[strip(q), stripe(k)],
            send_sem=asend.at[k, q],
            recv_sem=srecv.at[k, q],
            device_id={"space": device},
            device_id_type=MESH,
        )

    lends = at_end & (t == nt - 1)
    chunks = width // chunk

    scouted = (3 * chunks + 3) // 4

    @pl.when(lends)
    def _():
        for k in range(scouted):
            for q in range(PARTS):
                lend(k, q, scout).start()

    order = list(range(cap - 1, -1, -1))
    length = len_ref[0]

    def block_of(slot, r, cols):
        if tile <= share:
            part, at = divmod(r, share)
            owner, part = divmod(part, parts)
            return full[slot, owner, part, at : at + tile, cols]
        if tile <= rows:
            owner, at = divmod(r, rows)
            part, count = at // share, tile // share
            block = full[slot, owner, part : part + count, :, cols]
        else:
            block = full[slot, r // rows : (r + tile) // rows, :, :, cols]
        return block.reshape(tile, block.shape[-1])

    def days(k, source, result, arrive, depart):
        columns = stripe(k)
        for slot in order:
            before = source.at[:, columns] if slot == cap - 1 else result.at[slot + 1, :, columns]
            stages = PARTS if slot == cap - 1 else 1
            depth = nodes // stages
            for q in range(stages):
                if slot == cap - 1:
                    arrive(q)
                span_q = slice(q * depth, (q + 1) * depth)
                operand = before[span_q, :]
                for r in range(0, nodes, tile):
                    value = jnp.dot(
                        block_of(slot, r, span_q), operand, preferred_element_type=jnp.float32
                    )
                    if q > 0:
                        value = total[r : r + tile, :] + value
                    if q < stages - 1:
                        total[r : r + tile, :] = value
                        continue
                    kept = before[r : r + tile, :].astype(jnp.float32)
                    value = jnp.where(slot < length, value, kept)
                    result[slot, r : r + tile, columns] = value.astype(result.dtype)
                    if slot == 0 and (r + tile) % half == 0:
                        depart(r // half)

    @pl.when(t == nt - 1)
    def _():
        carry[...] = anchor_ref[...]

    def hop(slot, s, way):
        owner = z - way * s
        d = (1 - way) // 2
        block = full.at[slot, owner]
        return pltpu.make_async_remote_copy(
            src_ref=steps_ref.at[slot] if s == 0 else block,
            dst_ref=block,
            send_sem=gsend.at[d, slot, s],
            recv_sem=grecv.at[d, slot, s],
            device_id={"space": z + way},
            device_id_type=MESH,
        )

    def sends(s, way):
        if way > 0:
            return (z >= s) & (z < nz - 1)
        return (z + s < nz) & (z > 0)

    def receives(s, way):
        return z - 1 >= s if way > 0 else z + 1 + s < nz

    def arrival(slot, s, way):
        owner = z - way * (s + 1)
        d = (1 - way) // 2
        block = full.at[slot, owner]
        return pltpu.make_async_remote_copy(
            src_ref=block,
            dst_ref=block,
            send_sem=gsend.at[d, slot, s],
            recv_sem=grecv.at[d, slot, s],
            device_id={"space": z - way},
            device_id_type=MESH,
        )

    def launch(slot, s):
        for way in (-1, 1):

            @pl.when(sends(s, way))
            def _():
                hop(slot, s, way).start()

    def forward(lane, s):
        for way in (-1, 1):

            @pl.when(receives(s, way))
            def _():
                arrival(lane, s, way).wait_recv()

            if s + 1 < nz - 1:

                @pl.when(sends(s + 1, way))
                def _():
                    hop(lane, s + 1, way).start()

    lanes = [0] if packed else order
    if packed:
        note, notes, known, held, mixed, lsend, lrecv, esend, erecv, dsend, drecv, hsends, hrecvs = spread[:13]
        pieces = held.shape[0]
        gift, land = spread[13 : 13 + pieces], spread[13 + pieces :]
        piece = share // pieces
        extra = cap - 1

        def link(j):
            if nt != 8:
                return j
            return jnp.where(lax.rem(t, 2) == 0, EVEN[j - 1], ODD[j - 1])

        def peer(j):
            if nt != 8:
                return lax.rem(t + j, nt)
            device, bit = 0, 1
            while bit < nt:
                mine, other = lax.rem(t // bit, 2), lax.rem(link(j) // bit, 2)
                device = device + bit * (mine + other - 2 * mine * other)
                bit *= 2
            return device

        def source(j):
            return lax.rem(t + nt - j, nt) if nt != 8 else peer(j)

        def tell(j, section):
            return pltpu.make_async_remote_copy(
                src_ref=note,
                dst_ref=notes.at[section],
                send_sem=lsend.at[link(j)],
                recv_sem=lrecv.at[link(j)],
                device_id={"tm": peer(j)},
                device_id_type=MESH,
            )

        def give(j, p, section):
            return pltpu.make_async_remote_copy(
                src_ref=steps_ref.at[1:cap, peer(j), p * piece : (p + 1) * piece],
                dst_ref=gift[p].at[pl.ds(section * extra, extra)],
                send_sem=esend.at[p, link(j)],
                recv_sem=erecv.at[p, link(j)],
                device_id={"tm": peer(j)},
                device_id_type=MESH,
            )

        def landing(p, s, way):
            return land[((1 - way) // 2 * (nz - 1) + s) * pieces + p]

        def carry_on(p, s, way):
            d = (1 - way) // 2
            return pltpu.make_async_remote_copy(
                src_ref=held.at[p] if s == 0 else landing(p, s - 1, way),
                dst_ref=landing(p, s, way),
                send_sem=hsends.at[d, p, s],
                recv_sem=hrecvs.at[d, p, s],
                device_id={"space": z + way},
                device_id_type=MESH,
            )

        def lands(p, s, way):
            d = (1 - way) // 2
            return pltpu.make_async_remote_copy(
                src_ref=landing(p, s, way),
                dst_ref=landing(p, s, way),
                send_sem=hsends.at[d, p, s],
                recv_sem=hrecvs.at[d, p, s],
                device_id={"space": z - way},
                device_id_type=MESH,
            )

        def deal(j, p, s, way, carrier):
            d = (1 - way) // 2
            owner = z - way * (s + 1)
            return pltpu.make_async_remote_copy(
                src_ref=mixed.at[p, owner, peer(j)],
                dst_ref=full.at[1:cap, owner, carrier, p * piece : (p + 1) * piece],
                send_sem=dsend.at[d, p, s, link(j)],
                recv_sem=drecv.at[d, p, s, link(j)],
                device_id={"tm": peer(j)},
                device_id_type=MESH,
            )

        launch(0, 0)
        note[...] = jnp.full(note.shape, len_ref[0], jnp.int32)
        for j in range(1, nt):
            tell(j, t).start()
        for p in range(pieces):
            for j in range(1, nt):
                give(j, p, t).start()
        notes[t] = note[...]
        for p in range(pieces):
            for e in range(extra):
                gift[p][t * extra + e] = steps_ref[1 + e, t, p * piece : (p + 1) * piece]
        for j in range(1, nt):
            tell(j, source(j)).wait_recv()
        read = pltpu.make_async_copy(notes, known, lsend.at[0])
        read.start()
        read.wait()
        begin, ahead = [None] * nt, 0
        for section in range(nt - 1, -1, -1):
            begin[section] = ahead
            ahead = ahead + known[section, 0, 0] - 1
        picks = []
        for k in range(nt):
            pick = 0
            for section in range(nt):
                ahead = k - begin[section]
                mine = (ahead >= 0) & (ahead < known[section, 0, 0] - 1)
                pick = jnp.where(mine, section * extra + ahead, pick)
            picks.append(pick)
        for p in range(pieces):
            for j in range(1, nt):
                give(j, p, source(j)).wait_recv()
            for k in range(nt):
                held[p, k] = gift[p][picks[k]]
            for way in (-1, 1):

                @pl.when(sends(0, way))
                def _():
                    carry_on(p, 0, way).start()

        for slot in range(cap):
            full[slot, z] = steps_ref[slot]
        for s in range(nz - 1):
            for p in range(pieces):
                for way in (-1, 1):

                    @pl.when(receives(s, way))
                    def _():
                        lands(p, s, way).wait_recv()

                    if s + 1 < nz - 1:

                        @pl.when(sends(s + 1, way))
                        def _():
                            carry_on(p, s + 1, way).start()

                for way in (-1, 1):

                    @pl.when(receives(s, way))
                    def _():
                        owner = z - way * (s + 1)
                        for section in range(nt):
                            for e in range(extra):
                                k = jnp.clip(begin[section] + e, 0, nt - 1)
                                mixed[p, owner, section, e] = landing(p, s, way)[k]
                        for j in range(1, nt):
                            deal(j, p, s, way, t).start()
                        for e in range(extra):
                            full[1 + e, owner, t, p * piece : (p + 1) * piece] = mixed[p, owner, t, e]

            forward(0, s)

        for s in range(nz - 1):
            for way in (-1, 1):

                @pl.when(receives(s, way))
                def _():
                    for p in range(pieces):
                        for j in range(1, nt):
                            deal(j, p, s, way, source(j)).wait_recv()
    else:
        launch(order[0], 0)
        for i, slot in enumerate(order):
            if i + 1 < cap:
                launch(order[i + 1], 0)
            full[slot, z] = steps_ref[slot]
            for s in range(nz - 1):
                forward(slot, s)

    def pass_on(k, q, device):
        return pltpu.make_async_remote_copy(
            src_ref=out_ref.at[0, strip(q), stripe(k)],
            dst_ref=carry.at[strip(q), stripe(k)],
            send_sem=csend.at[k, q],
            recv_sem=crecv.at[k, q],
            device_id={"tm": device},
            device_id_type=MESH,
        )

    def scout_on(k, q, device):
        return pltpu.make_async_remote_copy(
            src_ref=scout_out.at[0, strip(q), stripe(k)],
            dst_ref=scout_in.at[strip(q), stripe(k)],
            send_sem=ssend.at[k, q],
            recv_sem=srecv.at[k, q],
            device_id={"tm": device},
            device_id_type=MESH,
        )

    def hand_over(k, q):
        return pltpu.make_async_remote_copy(
            src_ref=scout_out.at[0, strip(q), stripe(k)],
            dst_ref=carry.at[strip(q), stripe(k)],
            send_sem=hsend.at[k, q],
            recv_sem=crecv.at[k, q],
            device_id={"tm": t - 1, "space": end},
            device_id_type=MESH,
        )

    @pl.when(scouts & (t >= span))
    def _():
        def scout_chunk(k, _):
            def arrive(q):
                scout_on(k, q, t - 1).wait_recv()

            def depart(q):
                @pl.when(crossed)
                def _():
                    hand_over(k, q).start()

                @pl.when(t > span)
                def _():
                    scout_on(k, q, t - 1).start()

            days(k, scout_in, scout_out, arrive, depart)
            return 0

        lax.fori_loop(0, scouted, scout_chunk, 0)

    given = at_end & crossed
    turn = jnp.where(at_end & (t >= nt - 2 * span), scouted, 0)

    def store(k):
        return pltpu.make_async_copy(
            out_ref.at[:, :, stripe(k)], out_far.at[:, :, stripe(k)], stores.at[k]
        )

    def one_chunk(j, _):
        k = lax.rem(j + turn, chunks)

        def arrive(q):
            @pl.when(t < nt - 1)
            def _():
                pass_on(k, q, t + 1).wait_recv()

        def depart(q):
            @pl.when((t > 0) & jnp.logical_not(given & (k < scouted)))
            def _():
                pass_on(k, q, t - 1).start()

        days(k, carry, out_ref, arrive, depart)
        store(k).start()
        return 0

    lax.fori_loop(0, chunks, one_chunk, 0)
    for k in range(chunks):
        store(k).wait()

    @pl.when(lends)
    def _():
        for k in range(scouted):
            for q in range(PARTS):
                lend(k, q, scout).wait_send()

    @pl.when(scouts & (t > span))
    def _():
        for k in range(scouted):
            for q in range(PARTS):
                scout_on(k, q, t - 1).wait_send()

    @pl.when(gives)
    def _():
        for k in range(scouted):
            for q in range(PARTS):
                hand_over(k, q).wait_send()

    for lane in lanes:
        for s in range(nz - 1):
            for way in (-1, 1):

                @pl.when(sends(s, way))
                def _():
                    hop(lane, s, way).wait_send()

    if packed:
        for j in range(1, nt):
            tell(j, t).wait_send()
            for p in range(pieces):
                give(j, p, t).wait_send()
        for s in range(nz - 1):
            for way in (-1, 1):
                for p in range(pieces):

                    @pl.when(sends(s, way))
                    def _():
                        carry_on(p, s, way).wait_send()

                    @pl.when(receives(s, way))
                    def _():
                        for j in range(1, nt):
                            deal(j, p, s, way, t).wait_send()

    for k in range(chunks):
        kept = given if k < scouted else False

        @pl.when((t > 0) & jnp.logical_not(kept))
        def _():
            for q in range(PARTS):
                pass_on(k, q, t - 1).wait_send()


def widen(len_ref, panels_ref, out_ref, narrow, wide, loads, sems):
    cap, nodes, _ = panels_ref.shape
    depth = min(TILE, nodes)
    blocks = [
        (slot, i, pl.ds(r, depth)) for slot in range(cap) for i, r in enumerate(range(0, nodes, depth))
    ]

    def fetch(slot, i, rows):
        return pltpu.make_async_copy(
            panels_ref.at[slot, rows], narrow.at[slot, rows], loads.at[slot, i]
        )

    def put(slot, i, rows):
        return pltpu.make_async_copy(wide.at[slot, rows], out_ref.at[slot, rows], sems.at[slot, i])

    for block in blocks:
        fetch(*block).start()
    for slot, i, rows in blocks:
        fetch(slot, i, rows).wait()
        value = narrow[slot, rows, :].astype(jnp.float32)
        wide[slot, rows, :] = jnp.where(slot < len_ref[0], value, 0.0)
        put(slot, i, rows).start()
    for block in blocks:
        put(*block).wait()


def shards(nt, nz, steps, lengths, anchor):
    cap, rows, nodes = steps.shape
    width = anchor.shape[1]
    packed = cap == 3 and rows % (16 * nt) == 0
    parts = nt if packed else 1
    share, extra = rows // parts, cap - 1
    steps = steps.reshape(cap, parts, share, nodes)
    pieces = 2 if share % 32 == 0 else 1
    piece = share // pieces
    vmem16 = lambda *shape: pltpu.VMEM(shape, jnp.bfloat16)
    dma = pltpu.SemaphoreType.DMA
    spread = [
        pltpu.VMEM((8, 128), jnp.int32),
        pltpu.VMEM((nt, 8, 128), jnp.int32),
        pltpu.SMEM((nt, 8, 128), jnp.int32),
        vmem16(pieces, nt, piece, nodes),
        vmem16(pieces, nz, nt, extra, piece, nodes),
        dma((nt,)),
        dma((nt,)),
        dma((pieces, nt)),
        dma((pieces, nt)),
        dma((2, pieces, nz - 1, nt)),
        dma((2, pieces, nz - 1, nt)),
        dma((2, pieces, nz - 1)),
        dma((2, pieces, nz - 1)),
        *[vmem16(nt * extra, piece, nodes)] * pieces,
        *[vmem16(nt, piece, nodes)] * (2 * (nz - 1) * pieces),
    ]
    chunks = width // min(CHUNK, width)
    far = pl.BlockSpec(memory_space=pltpu.HBM)
    panels = pl.pallas_call(
        functools.partial(kernel, nt, nz),
        out_shape=jax.ShapeDtypeStruct((cap, nodes, width), jnp.bfloat16),
        in_specs=[pl.BlockSpec(memory_space=pltpu.SMEM), far, far],
        out_specs=far,
        scratch_shapes=[
            pltpu.VMEM((cap, nodes, width), jnp.bfloat16),
            pltpu.SemaphoreType.DMA((chunks,)),
            pltpu.VMEM(steps.shape, jnp.bfloat16),
            pltpu.VMEM(anchor.shape, jnp.bfloat16),
            pltpu.SemaphoreType.DMA((2,)),
            pltpu.VMEM((cap, nz, parts, share, nodes), jnp.bfloat16),
            pltpu.VMEM((nodes, width), jnp.bfloat16),
            pltpu.VMEM((cap, nodes, width), jnp.bfloat16),
            pltpu.VMEM((nodes, width), jnp.bfloat16),
            pltpu.VMEM((nodes, min(CHUNK, width)), jnp.float32),
            pltpu.SemaphoreType.DMA((2, cap, nz - 1)),
            pltpu.SemaphoreType.DMA((2, cap, nz - 1)),
            pltpu.SemaphoreType.DMA((chunks, PARTS)),
            pltpu.SemaphoreType.DMA((chunks, PARTS)),
            pltpu.SemaphoreType.DMA((chunks, PARTS)),
            pltpu.SemaphoreType.DMA((chunks, PARTS)),
            pltpu.SemaphoreType.DMA((chunks, PARTS)),
            pltpu.SemaphoreType.DMA((chunks, PARTS)),
            *(spread if packed else []),
        ],
        compiler_params=pltpu.CompilerParams(
            collective_id=0, has_side_effects=True, vmem_limit_bytes=GRANT
        ),
    )(lengths, steps, anchor)
    shape = (cap, nodes, width)
    return pl.pallas_call(
        widen,
        out_shape=jax.ShapeDtypeStruct(shape, jnp.float32),
        in_specs=[pl.BlockSpec(memory_space=pltpu.SMEM), far],
        out_specs=pl.BlockSpec(memory_space=pl.ANY),
        scratch_shapes=[
            pltpu.VMEM(shape, jnp.bfloat16),
            pltpu.VMEM(shape, jnp.float32),
            pltpu.SemaphoreType.DMA((cap, nodes // min(TILE, nodes))),
            pltpu.SemaphoreType.DMA((cap, nodes // min(TILE, nodes))),
        ],
        compiler_params=pltpu.CompilerParams(vmem_limit_bytes=GRANT),
    )(lengths, panels)


def solution(mesh):
    return jax.shard_map(
        functools.partial(shards, mesh.shape["tm"], mesh.shape["space"]),
        mesh=mesh,
        in_specs=(P("tm", "space", None), P("tm"), P(None, "space")),
        out_specs=P("tm", None, "space"),
        check_vma=False,
    )
```

```python
import functools

import jax
import jax.numpy as jnp
from jax import lax
from jax.experimental import pallas as pl
from jax.experimental.pallas import tpu as pltpu
from jax.sharding import PartitionSpec as P

MESH = pl.DeviceIdType.MESH
CHUNK = 128
TILE = 256
SPANS = 4
PARTS = 2
EVEN = (6, 7, 2, 5, 3, 4, 1)
ODD = (6, 7, 4, 3, 5, 2, 1)
GRANT = 60 << 20


def kernel(
    nt, nz, len_ref, steps_far, anchor_far, out_far, out_ref, stores, steps_ref, anchor_ref, loads, full, carry, scout_out, scout_in,
    total, gsend, grecv, csend, crecv, ssend, srecv, asend, hsend, *spread
):
    t, z = lax.axis_index("tm"), lax.axis_index("space")
    cap, parts, share, nodes = steps_ref.shape
    rows = parts * share
    packed = bool(spread)
    width = anchor_ref.shape[1]
    chunk = min(CHUNK, width)
    tile = min(TILE, nodes)

    fetches = [
        pltpu.make_async_copy(steps_far, steps_ref, loads.at[0]),
        pltpu.make_async_copy(anchor_far, anchor_ref, loads.at[1]),
    ]
    for fetch in fetches:
        fetch.start()

    barrier = pltpu.get_barrier_semaphore()
    near = {"tm": range(1, nt) if packed else (1, nt - 1), "space": (1, nz - 1)}
    for axis, at, size in (("tm", t, nt), ("space", z, nz)):
        for step in near[axis]:
            pl.semaphore_signal(
                barrier,
                inc=1,
                device_id={axis: lax.rem(at + step, size)},
                device_id_type=MESH,
            )
    span = max(1, nt // SPANS)
    at_end = (z == 0) | (z == nz - 1)
    scouts = (z == 1) | (z == nz - 2)
    end = jnp.where(z <= 1, 0, nz - 1)
    scout = jnp.where(z <= 1, 1, nz - 2)
    edge = lax.rem(t, span) == 0
    crossed = edge & (t > 0) & (t < nt - span)
    gives = scouts & crossed
    takes = at_end & (lax.rem(t, span) == span - 1) & (t < nt - 1 - span)

    @pl.when(gives)
    def _():
        pl.semaphore_signal(
            barrier,
            inc=1,
            device_id={"tm": t - 1, "space": end},
            device_id_type=MESH,
        )

    @pl.when(takes)
    def _():
        pl.semaphore_signal(
            barrier,
            inc=1,
            device_id={"tm": t + 1, "space": scout},
            device_id_type=MESH,
        )

    greeted = len(near["tm"]) + len(near["space"])
    pl.semaphore_wait(barrier, greeted + jnp.where(gives | takes, 1, 0))
    for fetch in fetches:
        fetch.wait()

    def stripe(k):
        return pl.ds(pl.multiple_of(k * chunk, chunk), chunk)

    half = nodes // PARTS

    def strip(q):
        return pl.ds(q * half, half)

    def lend(k, q, device):
        return pltpu.make_async_remote_copy(
            src_ref=anchor_ref.at[strip(q), stripe(k)],
            dst_ref=scout_in.at[strip(q), stripe(k)],
            send_sem=asend.at[k, q],
            recv_sem=srecv.at[k, q],
            device_id={"space": device},
            device_id_type=MESH,
        )

    lends = at_end & (t == nt - 1)
    chunks = width // chunk

    scouted = (3 * chunks + 3) // 4

    @pl.when(lends)
    def _():
        for k in range(scouted):
            for q in range(PARTS):
                lend(k, q, scout).start()

    order = list(range(cap - 1, -1, -1))
    length = len_ref[0]

    def block_of(slot, r, cols):
        if tile <= share:
            part, at = divmod(r, share)
            owner, part = divmod(part, parts)
            return full[slot, owner, part, at : at + tile, cols]
        if tile <= rows:
            owner, at = divmod(r, rows)
            part, count = at // share, tile // share
            block = full[slot, owner, part : part + count, :, cols]
        else:
            block = full[slot, r // rows : (r + tile) // rows, :, :, cols]
        return block.reshape(tile, block.shape[-1])

    def days(k, source, result, arrive, depart):
        columns = stripe(k)
        for slot in order:
            before = source.at[:, columns] if slot == cap - 1 else result.at[slot + 1, :, columns]
            stages = PARTS if slot == cap - 1 else 1
            depth = nodes // stages
            for q in range(stages):
                if slot == cap - 1:
                    arrive(q)
                span_q = slice(q * depth, (q + 1) * depth)
                operand = before[span_q, :]
                for r in range(0, nodes, tile):
                    value = jnp.dot(
                        block_of(slot, r, span_q), operand, preferred_element_type=jnp.float32
                    )
                    if q > 0:
                        value = total[r : r + tile, :] + value
                    if q < stages - 1:
                        total[r : r + tile, :] = value
                        continue
                    kept = before[r : r + tile, :].astype(jnp.float32)
                    value = jnp.where(slot < length, value, kept)
                    result[slot, r : r + tile, columns] = value.astype(result.dtype)
                    if slot == 0 and (r + tile) % half == 0:
                        depart(r // half)

    @pl.when(t == nt - 1)
    def _():
        carry[...] = anchor_ref[...]

    def hop(slot, s, way):
        owner = z - way * s
        d = (1 - way) // 2
        block = full.at[slot, owner]
        return pltpu.make_async_remote_copy(
            src_ref=steps_ref.at[slot] if s == 0 else block,
            dst_ref=block,
            send_sem=gsend.at[d, slot, s],
            recv_sem=grecv.at[d, slot, s],
            device_id={"space": z + way},
            device_id_type=MESH,
        )

    def sends(s, way):
        if way > 0:
            return (z >= s) & (z < nz - 1)
        return (z + s < nz) & (z > 0)

    def receives(s, way):
        return z - 1 >= s if way > 0 else z + 1 + s < nz

    def arrival(slot, s, way):
        owner = z - way * (s + 1)
        d = (1 - way) // 2
        block = full.at[slot, owner]
        return pltpu.make_async_remote_copy(
            src_ref=block,
            dst_ref=block,
            send_sem=gsend.at[d, slot, s],
            recv_sem=grecv.at[d, slot, s],
            device_id={"space": z - way},
            device_id_type=MESH,
        )

    def launch(slot, s):
        for way in (-1, 1):

            @pl.when(sends(s, way))
            def _():
                hop(slot, s, way).start()

    def forward(lane, s):
        for way in (-1, 1):

            @pl.when(receives(s, way))
            def _():
                arrival(lane, s, way).wait_recv()

            if s + 1 < nz - 1:

                @pl.when(sends(s + 1, way))
                def _():
                    hop(lane, s + 1, way).start()

    lanes = [0] if packed else order
    if packed:
        note, notes, known, held, mixed, lsend, lrecv, esend, erecv, dsend, drecv, hsends, hrecvs = spread[:13]
        pieces = held.shape[0]
        gift, land = spread[13 : 13 + pieces], spread[13 + pieces :]
        piece = share // pieces
        extra = cap - 1

        def link(j):
            if nt != 8:
                return j
            return jnp.where(lax.rem(t, 2) == 0, EVEN[j - 1], ODD[j - 1])

        def peer(j):
            if nt != 8:
                return lax.rem(t + j, nt)
            device, bit = 0, 1
            while bit < nt:
                mine, other = lax.rem(t // bit, 2), lax.rem(link(j) // bit, 2)
                device = device + bit * (mine + other - 2 * mine * other)
                bit *= 2
            return device

        def source(j):
            return lax.rem(t + nt - j, nt) if nt != 8 else peer(j)

        def tell(j, section):
            return pltpu.make_async_remote_copy(
                src_ref=note,
                dst_ref=notes.at[section],
                send_sem=lsend.at[link(j)],
                recv_sem=lrecv.at[link(j)],
                device_id={"tm": peer(j)},
                device_id_type=MESH,
            )

        def give(j, p, section):
            return pltpu.make_async_remote_copy(
                src_ref=steps_ref.at[1:cap, peer(j), p * piece : (p + 1) * piece],
                dst_ref=gift[p].at[pl.ds(section * extra, extra)],
                send_sem=esend.at[p, link(j)],
                recv_sem=erecv.at[p, link(j)],
                device_id={"tm": peer(j)},
                device_id_type=MESH,
            )

        def landing(p, s, way):
            return land[((1 - way) // 2 * (nz - 1) + s) * pieces + p]

        def carry_on(p, s, way):
            d = (1 - way) // 2
            return pltpu.make_async_remote_copy(
                src_ref=held.at[p] if s == 0 else landing(p, s - 1, way),
                dst_ref=landing(p, s, way),
                send_sem=hsends.at[d, p, s],
                recv_sem=hrecvs.at[d, p, s],
                device_id={"space": z + way},
                device_id_type=MESH,
            )

        def lands(p, s, way):
            d = (1 - way) // 2
            return pltpu.make_async_remote_copy(
                src_ref=landing(p, s, way),
                dst_ref=landing(p, s, way),
                send_sem=hsends.at[d, p, s],
                recv_sem=hrecvs.at[d, p, s],
                device_id={"space": z - way},
                device_id_type=MESH,
            )

        def deal(j, p, s, way, carrier):
            d = (1 - way) // 2
            owner = z - way * (s + 1)
            return pltpu.make_async_remote_copy(
                src_ref=mixed.at[p, owner, peer(j)],
                dst_ref=full.at[1:cap, owner, carrier, p * piece : (p + 1) * piece],
                send_sem=dsend.at[d, p, s, link(j)],
                recv_sem=drecv.at[d, p, s, link(j)],
                device_id={"tm": peer(j)},
                device_id_type=MESH,
            )

        launch(0, 0)
        note[...] = jnp.full(note.shape, len_ref[0], jnp.int32)
        for j in range(1, nt):
            tell(j, t).start()
        for p in range(pieces):
            for j in range(1, nt):
                give(j, p, t).start()
        notes[t] = note[...]
        for p in range(pieces):
            for e in range(extra):
                gift[p][t * extra + e] = steps_ref[1 + e, t, p * piece : (p + 1) * piece]
        for j in range(1, nt):
            tell(j, source(j)).wait_recv()
        read = pltpu.make_async_copy(notes, known, lsend.at[0])
        read.start()
        read.wait()
        begin, ahead = [None] * nt, 0
        for section in range(nt - 1, -1, -1):
            begin[section] = ahead
            ahead = ahead + known[section, 0, 0] - 1
        picks = []
        for k in range(nt):
            pick = 0
            for section in range(nt):
                ahead = k - begin[section]
                mine = (ahead >= 0) & (ahead < known[section, 0, 0] - 1)
                pick = jnp.where(mine, section * extra + ahead, pick)
            picks.append(pick)
        for p in range(pieces):
            for j in range(1, nt):
                give(j, p, source(j)).wait_recv()
            for k in range(nt):
                held[p, k] = gift[p][picks[k]]
            for way in (-1, 1):

                @pl.when(sends(0, way))
                def _():
                    carry_on(p, 0, way).start()

        for slot in range(cap):
            full[slot, z] = steps_ref[slot]
        for s in range(nz - 1):
            for p in range(pieces):
                for way in (-1, 1):

                    @pl.when(receives(s, way))
                    def _():
                        lands(p, s, way).wait_recv()

                    if s + 1 < nz - 1:

                        @pl.when(sends(s + 1, way))
                        def _():
                            carry_on(p, s + 1, way).start()

                for way in (-1, 1):

                    @pl.when(receives(s, way))
                    def _():
                        owner = z - way * (s + 1)
                        for section in range(nt):
                            for e in range(extra):
                                k = jnp.clip(begin[section] + e, 0, nt - 1)
                                mixed[p, owner, section, e] = landing(p, s, way)[k]
                        for j in range(1, nt):
                            deal(j, p, s, way, t).start()
                        for e in range(extra):
                            full[1 + e, owner, t, p * piece : (p + 1) * piece] = mixed[p, owner, t, e]

            forward(0, s)

        for s in range(nz - 1):
            for way in (-1, 1):

                @pl.when(receives(s, way))
                def _():
                    for p in range(pieces):
                        for j in range(1, nt):
                            deal(j, p, s, way, source(j)).wait_recv()
    else:
        launch(order[0], 0)
        for i, slot in enumerate(order):
            if i + 1 < cap:
                launch(order[i + 1], 0)
            full[slot, z] = steps_ref[slot]
            for s in range(nz - 1):
                forward(slot, s)

    def pass_on(k, q, device):
        return pltpu.make_async_remote_copy(
            src_ref=out_ref.at[0, strip(q), stripe(k)],
            dst_ref=carry.at[strip(q), stripe(k)],
            send_sem=csend.at[k, q],
            recv_sem=crecv.at[k, q],
            device_id={"tm": device},
            device_id_type=MESH,
        )

    def scout_on(k, q, device):
        return pltpu.make_async_remote_copy(
            src_ref=scout_out.at[0, strip(q), stripe(k)],
            dst_ref=scout_in.at[strip(q), stripe(k)],
            send_sem=ssend.at[k, q],
            recv_sem=srecv.at[k, q],
            device_id={"tm": device},
            device_id_type=MESH,
        )

    def hand_over(k, q):
        return pltpu.make_async_remote_copy(
            src_ref=scout_out.at[0, strip(q), stripe(k)],
            dst_ref=carry.at[strip(q), stripe(k)],
            send_sem=hsend.at[k, q],
            recv_sem=crecv.at[k, q],
            device_id={"tm": t - 1, "space": end},
            device_id_type=MESH,
        )

    @pl.when(scouts & (t >= span))
    def _():
        def scout_chunk(k, _):
            def arrive(q):
                scout_on(k, q, t - 1).wait_recv()

            def depart(q):
                @pl.when(crossed)
                def _():
                    hand_over(k, q).start()

                @pl.when(t > span)
                def _():
                    scout_on(k, q, t - 1).start()

            days(k, scout_in, scout_out, arrive, depart)
            return 0

        lax.fori_loop(0, scouted, scout_chunk, 0)

    given = at_end & crossed
    turn = jnp.where(at_end & (t >= nt - 2 * span), scouted, 0)

    def store(k):
        return pltpu.make_async_copy(
            out_ref.at[:, :, stripe(k)], out_far.at[:, :, stripe(k)], stores.at[k]
        )

    def one_chunk(j, _):
        k = lax.rem(j + turn, chunks)

        def arrive(q):
            @pl.when(t < nt - 1)
            def _():
                pass_on(k, q, t + 1).wait_recv()

        def depart(q):
            @pl.when((t > 0) & jnp.logical_not(given & (k < scouted)))
            def _():
                pass_on(k, q, t - 1).start()

        days(k, carry, out_ref, arrive, depart)
        store(k).start()
        return 0

    lax.fori_loop(0, chunks, one_chunk, 0)
    for k in range(chunks):
        store(k).wait()

    @pl.when(lends)
    def _():
        for k in range(scouted):
            for q in range(PARTS):
                lend(k, q, scout).wait_send()

    @pl.when(scouts & (t > span))
    def _():
        for k in range(scouted):
            for q in range(PARTS):
                scout_on(k, q, t - 1).wait_send()

    @pl.when(gives)
    def _():
        for k in range(scouted):
            for q in range(PARTS):
                hand_over(k, q).wait_send()

    for lane in lanes:
        for s in range(nz - 1):
            for way in (-1, 1):

                @pl.when(sends(s, way))
                def _():
                    hop(lane, s, way).wait_send()

    if packed:
        for j in range(1, nt):
            tell(j, t).wait_send()
            for p in range(pieces):
                give(j, p, t).wait_send()
        for s in range(nz - 1):
            for way in (-1, 1):
                for p in range(pieces):

                    @pl.when(sends(s, way))
                    def _():
                        carry_on(p, s, way).wait_send()

                    @pl.when(receives(s, way))
                    def _():
                        for j in range(1, nt):
                            deal(j, p, s, way, t).wait_send()

    for k in range(chunks):
        kept = given if k < scouted else False

        @pl.when((t > 0) & jnp.logical_not(kept))
        def _():
            for q in range(PARTS):
                pass_on(k, q, t - 1).wait_send()


def widen(len_ref, panels_ref, out_ref, narrow, wide, loads, sems):
    cap, nodes, _ = panels_ref.shape
    depth = min(TILE // 2, nodes)
    blocks = [
        (slot, i, pl.ds(r, depth)) for slot in range(cap) for i, r in enumerate(range(0, nodes, depth))
    ]

    def fetch(slot, i, rows):
        return pltpu.make_async_copy(
            panels_ref.at[slot, rows], narrow.at[slot, rows], loads.at[slot, i]
        )

    def put(slot, i, rows):
        return pltpu.make_async_copy(wide.at[slot, rows], out_ref.at[slot, rows], sems.at[slot, i])

    for block in blocks:
        fetch(*block).start()
    for slot, i, rows in blocks:
        fetch(slot, i, rows).wait()
        value = narrow[slot, rows, :].astype(jnp.float32)
        wide[slot, rows, :] = jnp.where(slot < len_ref[0], value, 0.0)
        put(slot, i, rows).start()
    for block in blocks:
        put(*block).wait()


def shards(nt, nz, steps, lengths, anchor):
    cap, rows, nodes = steps.shape
    width = anchor.shape[1]
    packed = cap == 3 and rows % (16 * nt) == 0
    parts = nt if packed else 1
    share, extra = rows // parts, cap - 1
    steps = steps.reshape(cap, parts, share, nodes)
    pieces = 2 if share % 32 == 0 else 1
    piece = share // pieces
    vmem16 = lambda *shape: pltpu.VMEM(shape, jnp.bfloat16)
    dma = pltpu.SemaphoreType.DMA
    spread = [
        pltpu.VMEM((8, 128), jnp.int32),
        pltpu.VMEM((nt, 8, 128), jnp.int32),
        pltpu.SMEM((nt, 8, 128), jnp.int32),
        vmem16(pieces, nt, piece, nodes),
        vmem16(pieces, nz, nt, extra, piece, nodes),
        dma((nt,)),
        dma((nt,)),
        dma((pieces, nt)),
        dma((pieces, nt)),
        dma((2, pieces, nz - 1, nt)),
        dma((2, pieces, nz - 1, nt)),
        dma((2, pieces, nz - 1)),
        dma((2, pieces, nz - 1)),
        *[vmem16(nt * extra, piece, nodes)] * pieces,
        *[vmem16(nt, piece, nodes)] * (2 * (nz - 1) * pieces),
    ]
    chunks = width // min(CHUNK, width)
    far = pl.BlockSpec(memory_space=pltpu.HBM)
    panels = pl.pallas_call(
        functools.partial(kernel, nt, nz),
        out_shape=jax.ShapeDtypeStruct((cap, nodes, width), jnp.bfloat16),
        in_specs=[pl.BlockSpec(memory_space=pltpu.SMEM), far, far],
        out_specs=far,
        scratch_shapes=[
            pltpu.VMEM((cap, nodes, width), jnp.bfloat16),
            pltpu.SemaphoreType.DMA((chunks,)),
            pltpu.VMEM(steps.shape, jnp.bfloat16),
            pltpu.VMEM(anchor.shape, jnp.bfloat16),
            pltpu.SemaphoreType.DMA((2,)),
            pltpu.VMEM((cap, nz, parts, share, nodes), jnp.bfloat16),
            pltpu.VMEM((nodes, width), jnp.bfloat16),
            pltpu.VMEM((cap, nodes, width), jnp.bfloat16),
            pltpu.VMEM((nodes, width), jnp.bfloat16),
            pltpu.VMEM((nodes, min(CHUNK, width)), jnp.float32),
            pltpu.SemaphoreType.DMA((2, cap, nz - 1)),
            pltpu.SemaphoreType.DMA((2, cap, nz - 1)),
            pltpu.SemaphoreType.DMA((chunks, PARTS)),
            pltpu.SemaphoreType.DMA((chunks, PARTS)),
            pltpu.SemaphoreType.DMA((chunks, PARTS)),
            pltpu.SemaphoreType.DMA((chunks, PARTS)),
            pltpu.SemaphoreType.DMA((chunks, PARTS)),
            pltpu.SemaphoreType.DMA((chunks, PARTS)),
            *(spread if packed else []),
        ],
        compiler_params=pltpu.CompilerParams(
            collective_id=0, has_side_effects=True, vmem_limit_bytes=GRANT
        ),
    )(lengths, steps, anchor)
    shape = (cap, nodes, width)
    return pl.pallas_call(
        widen,
        out_shape=jax.ShapeDtypeStruct(shape, jnp.float32),
        in_specs=[pl.BlockSpec(memory_space=pltpu.SMEM), far],
        out_specs=pl.BlockSpec(memory_space=pl.ANY),
        scratch_shapes=[
            pltpu.VMEM(shape, jnp.bfloat16),
            pltpu.VMEM(shape, jnp.float32),
            pltpu.SemaphoreType.DMA((cap, nodes // min(TILE // 2, nodes))),
            pltpu.SemaphoreType.DMA((cap, nodes // min(TILE // 2, nodes))),
        ],
        compiler_params=pltpu.CompilerParams(vmem_limit_bytes=GRANT),
    )(lengths, panels)


def solution(mesh):
    return jax.shard_map(
        functools.partial(shards, mesh.shape["tm"], mesh.shape["space"]),
        mesh=mesh,
        in_specs=(P("tm", "space", None), P("tm"), P(None, "space")),
        out_specs=P("tm", None, "space"),
        check_vma=False,
    )
```
